32 devices in a mesh: lat: 4 (over y, x), lon: 8 (over z, core).
Axes of the slice: x: 2, y: 2, z: 4, core: 2. Of those that a mesh axis runs over, the one named last changes fastest.
Arguments:
- fields: bfloat16 [1, 64, 64, 768], P(None, 'lat', 'lon'), may hold values from -6 to 6
- spec_cotangent: bfloat16 [2, 1, 64, 32, 768], P(None, None, 'lon', 'lat'), may hold values from -6 to 6
- inner_kernel: bfloat16 [2, 8, 96, 96], replicated, may hold values from -0.4375 to 0.4375
- inner_offset: float32 [2, 8, 96], replicated, may hold values from -3 to 3
- outer_kernel: bfloat16 [2, 8, 96, 96], replicated, may hold values from -0.4375 to 0.4375
- outer_offset: float32 [2, 8, 96], replicated, may hold values from -3 to 3
Outputs:
- filtered: float32 [2, 1, 64, 32, 768], P(None, None, 'lon', 'lat')
- inner_kernel_grad: float32 [2, 8, 96, 96], replicated
- inner_offset_grad: float32 [2, 8, 96], replicated
- outer_kernel_grad: float32 [2, 8, 96, 96], replicated
- outer_offset_grad: float32 [2, 8, 96], replicated
The draws below stay inside these ranges and needn't reach their ends.
All inputs are finite; a program needn't handle non-finite values.
Results may differ from the reference program's by a relative error of at most 0.0072.
Values may be sent and summed in bfloat16 or wider, within the bound.
A program may use at most 64 MiB of HBM per device.

```python
import math
import jax
import jax.numpy as jnp
from jax import lax

NB = 8
BS = 96
COND = 1
D = 768
H = 64
W = 64
KW = 32


def block_levels(own_key, shape, shards, least, top_value):
    loudness, own = 1.0, jax.random.fold_in(own_key, 6)
    for position, shards_of in shards:
        steps = jnp.exp(jax.random.uniform(jax.random.fold_in(own, position), (shards_of,), jnp.float32, least / len(shards), top_value / len(shards)))
        loudness = loudness * jnp.repeat(steps, shape[position] // shards_of).reshape([-1 if axis == position else 1 for axis in range(len(shape))])
    return loudness


def scatter_about(rng, shape, width, limit, split=(), held_as=jnp.bfloat16):
    result = width * jax.random.normal(rng, shape, jnp.float32)
    if split:
        result = result * block_levels(rng, shape, split, -0.22, 0.18)
    return jnp.clip(result, -limit, limit).astype(held_as)


def setup_inputs(seed: int = 0) -> dict:
    splits = jax.random.split(jax.random.key(seed), 7)
    return {
        "fields": scatter_about(splits[0], (COND, H, W, D), 1.0, 6.0, ((1, 4), (2, 8))),
        "spec_cotangent": scatter_about(splits[1], (2, COND, H, KW, D), 1.0, 6.0, ((2, 8), (3, 4))),
        "inner_kernel": scatter_about(splits[2], (2, NB, BS, BS), (2 * BS) ** -0.5, 0.4375),
        "inner_offset": scatter_about(splits[3], (2, NB, BS), 0.5, 3.0, (), jnp.float32),
        "outer_kernel": scatter_about(splits[4], (2, NB, BS, BS), (2 * BS) ** -0.5, 0.4375),
        "outer_offset": scatter_about(splits[5], (2, NB, BS), 0.5, 3.0, (), jnp.float32),
    }


shrink_level = 0.1
gelu_coeff = 0.7978845608028654
precise = lax.Precision.HIGHEST

def dft_tables(length, columns):
    points = jnp.arange(length, dtype=jnp.int32)
    orders = jnp.arange(columns, dtype=jnp.int32)
    product = points[:, None] * orders[None, :] % length
    angles = product.astype(jnp.float32) * (2.0 * math.pi / length)
    factor = 1.0 / math.sqrt(length)
    return (jnp.cos(angles) * factor, jnp.sin(angles) * factor)

def shrink(values):
    return values - shrink_level * jnp.tanh(values / shrink_level)

def shrink_slope(values):
    level = jnp.tanh(values / shrink_level)
    return level * level

def gelu_value(values):
    inner = gelu_coeff * (values + 0.044715 * values * values * values)
    return 0.5 * values * (1.0 + jnp.tanh(inner))

def gelu_slope(values):
    inner = gelu_coeff * (values + 0.044715 * values * values * values)
    level = jnp.tanh(inner)
    return 0.5 * (1.0 + level) + 0.5 * values * (1.0 - level * level) * gelu_coeff * (1.0 + 3.0 * 0.044715 * values * values)

def rounded(values):
    return lax.optimization_barrier(values.astype(jnp.bfloat16)).astype(jnp.float32)

def spectrum_of(field):
    floats = field.astype(jnp.float32)
    cosine_cols, sine_cols = dft_tables(W, KW)
    cosine_rows, sine_rows = dft_tables(H, H)
    half_real = jnp.einsum('hwc,wk->hkc', floats, cosine_cols, precision=precise)
    half_imag = -jnp.einsum('hwc,wk->hkc', floats, sine_cols, precision=precise)
    full_real = jnp.einsum('hkc,hm->mkc', half_real, cosine_rows, precision=precise) + jnp.einsum('hkc,hm->mkc', half_imag, sine_rows, precision=precise)
    full_imag = jnp.einsum('hkc,hm->mkc', half_imag, cosine_rows, precision=precise) - jnp.einsum('hkc,hm->mkc', half_real, sine_rows, precision=precise)
    return jnp.stack([full_real, full_imag]).astype(jnp.bfloat16)

def mixing(operand, kernel):
    return jnp.einsum('rnb,nbc->rnc', operand, kernel, precision=precise)

def backmix(operand, kernel):
    return jnp.einsum('rnc,nbc->rnb', operand, kernel, precision=precise)

def crossed(operand, second):
    return jnp.einsum('rnb,rnc->nbc', operand, second, precision=precise)

def block_filter(spectrum, cotangent, inner_kernel, inner_offset, outer_kernel, outer_offset):
    spec_real, spec_imag = (spectrum[0], spectrum[1])
    pre_real = mixing(spec_real, inner_kernel[0]) - mixing(spec_imag, inner_kernel[1]) + inner_offset[0]
    pre_imag = mixing(spec_imag, inner_kernel[0]) + mixing(spec_real, inner_kernel[1]) + inner_offset[1]
    hid_real = rounded(gelu_value(pre_real))
    hid_imag = rounded(gelu_value(pre_imag))
    out_real = mixing(hid_real, outer_kernel[0]) - mixing(hid_imag, outer_kernel[1]) + outer_offset[0]
    out_imag = mixing(hid_imag, outer_kernel[0]) + mixing(hid_real, outer_kernel[1]) + outer_offset[1]
    filtered = jnp.stack([shrink(out_real), shrink(out_imag)])
    back_real = rounded(cotangent[0] * shrink_slope(out_real))
    back_imag = rounded(cotangent[1] * shrink_slope(out_imag))
    outer_grad = jnp.stack([crossed(hid_real, back_real) + crossed(hid_imag, back_imag), crossed(hid_real, back_imag) - crossed(hid_imag, back_real)])
    outer_bias = jnp.stack([lax.optimization_barrier(jnp.sum(back_real, axis=0)), lax.optimization_barrier(jnp.sum(back_imag, axis=0))])
    grad_real = rounded((backmix(back_real, outer_kernel[0]) + backmix(back_imag, outer_kernel[1])) * gelu_slope(pre_real))
    grad_imag = rounded((backmix(back_imag, outer_kernel[0]) - backmix(back_real, outer_kernel[1])) * gelu_slope(pre_imag))
    inner_grad = jnp.stack([crossed(spec_real, grad_real) + crossed(spec_imag, grad_imag), crossed(spec_real, grad_imag) - crossed(spec_imag, grad_real)])
    inner_bias = jnp.stack([lax.optimization_barrier(jnp.sum(grad_real, axis=0)), lax.optimization_barrier(jnp.sum(grad_imag, axis=0))])
    return (filtered, (inner_grad, inner_bias, outer_grad, outer_bias))

def reference(fields, spec_cotangent, inner_kernel, inner_offset, outer_kernel, outer_offset):
    inner_floats = inner_kernel.astype(jnp.float32)
    outer_floats = outer_kernel.astype(jnp.float32)
    filtered_parts = []
    totals = None
    for condition in range(COND):
        spec_low = lax.optimization_barrier(spectrum_of(fields[condition]))
        spectrum = spec_low.astype(jnp.float32).reshape(2, H * KW, NB, BS)
        cotangent = spec_cotangent[:, condition].astype(jnp.float32).reshape(2, H * KW, NB, BS)
        filtered_block, gradients = block_filter(spectrum, cotangent, inner_floats, inner_offset, outer_floats, outer_offset)
        filtered_parts.append(filtered_block.reshape(2, H, KW, NB * BS))
        if totals is None:
            totals = gradients
        else:
            totals = tuple((first + second for first, second in zip(totals, gradients)))
    filtered = jnp.stack(filtered_parts, axis=1)
    normalizer = 1.0 / math.sqrt(COND * H * KW)
    return (filtered, totals[0] * normalizer, totals[1] * normalizer, totals[2] * normalizer, totals[3] * normalizer)
```

```python
import math

import jax
import jax.numpy as jnp
import numpy as np
from jax import lax
from jax.experimental import pallas as pl
from jax.experimental.pallas import tpu as pltpu
from jax.sharding import PartitionSpec as P

shrink_level = 0.1
gelu_coeff = 0.7978845608028654
precise = lax.Precision.HIGHEST


def dft_tables(length, columns):
    points = jnp.arange(length, dtype=jnp.int32)
    orders = jnp.arange(columns, dtype=jnp.int32)
    product = points[:, None] * orders[None, :] % length
    angles = product.astype(jnp.float32) * (2.0 * math.pi / length)
    factor = 1.0 / math.sqrt(length)
    return (jnp.cos(angles) * factor, jnp.sin(angles) * factor)


def shrink(values):
    return values - shrink_level * jnp.tanh(values / shrink_level)


def shrink_slope(values):
    level = jnp.tanh(values / shrink_level)
    return level * level


def gelu_value(values):
    inner = gelu_coeff * (values + 0.044715 * values * values * values)
    return 0.5 * values * (1.0 + jnp.tanh(inner))


def gelu_slope(values):
    inner = gelu_coeff * (values + 0.044715 * values * values * values)
    level = jnp.tanh(inner)
    return 0.5 * (1.0 + level) + 0.5 * values * (1.0 - level * level) * gelu_coeff * (
        1.0 + 3.0 * 0.044715 * values * values
    )


def mixing(operand, kernel):
    return jnp.einsum("rnb,nbc->rnc", operand, kernel, preferred_element_type=jnp.float32)


def backmix(operand, kernel):
    return jnp.einsum("rnc,nbc->rnb", operand, kernel, preferred_element_type=jnp.float32)


def crossed(operand, second):
    return jnp.einsum("rnb,rnc->nbc", operand, second, preferred_element_type=jnp.float32)


def block_filter(spectrum, cotangent, inner_kernel, inner_offset, outer_kernel, outer_offset):
    spec_real, spec_imag = (spectrum[0], spectrum[1])
    pre_real = (
        mixing(spec_real, inner_kernel[0]) - mixing(spec_imag, inner_kernel[1]) + inner_offset[0]
    )
    pre_imag = (
        mixing(spec_imag, inner_kernel[0]) + mixing(spec_real, inner_kernel[1]) + inner_offset[1]
    )
    hid_real = gelu_value(pre_real).astype(jnp.bfloat16)
    hid_imag = gelu_value(pre_imag).astype(jnp.bfloat16)
    out_real = (
        mixing(hid_real, outer_kernel[0]) - mixing(hid_imag, outer_kernel[1]) + outer_offset[0]
    )
    out_imag = (
        mixing(hid_imag, outer_kernel[0]) + mixing(hid_real, outer_kernel[1]) + outer_offset[1]
    )
    filtered = jnp.stack([shrink(out_real), shrink(out_imag)])
    back_real = (cotangent[0].astype(jnp.float32) * shrink_slope(out_real)).astype(jnp.bfloat16)
    back_imag = (cotangent[1].astype(jnp.float32) * shrink_slope(out_imag)).astype(jnp.bfloat16)
    outer_grad = jnp.stack(
        [
            crossed(hid_real, back_real) + crossed(hid_imag, back_imag),
            crossed(hid_real, back_imag) - crossed(hid_imag, back_real),
        ]
    )
    outer_bias = jnp.stack(
        [
            jnp.sum(back_real, axis=0, dtype=jnp.float32),
            jnp.sum(back_imag, axis=0, dtype=jnp.float32),
        ]
    )
    grad_real = (
        (backmix(back_real, outer_kernel[0]) + backmix(back_imag, outer_kernel[1]))
        * gelu_slope(pre_real)
    ).astype(jnp.bfloat16)
    grad_imag = (
        (backmix(back_imag, outer_kernel[0]) - backmix(back_real, outer_kernel[1]))
        * gelu_slope(pre_imag)
    ).astype(jnp.bfloat16)
    inner_grad = jnp.stack(
        [
            crossed(spec_real, grad_real) + crossed(spec_imag, grad_imag),
            crossed(spec_real, grad_imag) - crossed(spec_imag, grad_real),
        ]
    )
    inner_bias = jnp.stack(
        [
            jnp.sum(grad_real, axis=0, dtype=jnp.float32),
            jnp.sum(grad_imag, axis=0, dtype=jnp.float32),
        ]
    )
    return (filtered, (inner_grad, inner_bias, outer_grad, outer_bias))


def per_device(fields, spec_cotangent, inner_kernel, inner_offset, outer_kernel, outer_offset):
    lat_devices = lax.axis_size("lat")
    lon_devices = lax.axis_size("lon")
    conditions = fields.shape[0]
    height = fields.shape[1] * lat_devices
    width = fields.shape[2] * lon_devices
    wavenumbers = width // 2
    cosine_rows, sine_rows = dft_tables(height, height)
    cosine_cols, sine_cols = dft_tables(width, wavenumbers)
    arriving = lax.all_to_all(fields, "lat", split_axis=3, concat_axis=1, tiled=True)
    shape_in = arriving.shape
    floats = arriving.astype(jnp.float32).reshape(
        shape_in[0], shape_in[1], shape_in[2] * shape_in[3]
    )
    real_part = jnp.einsum("bhx,hm->bmx", floats, cosine_rows, precision=precise)
    imag_part = -jnp.einsum("bhx,hm->bmx", floats, sine_rows, precision=precise)
    spec_rows = jnp.stack([real_part, imag_part]).reshape((2,) + shape_in)
    arriving = lax.all_to_all(spec_rows, "lon", split_axis=2, concat_axis=3, tiled=True)
    real_part = jnp.einsum(
        "bhwd,wk->bhkd", arriving[0], cosine_cols, precision=precise
    ) + jnp.einsum("bhwd,wk->bhkd", arriving[1], sine_cols, precision=precise)
    imag_part = jnp.einsum(
        "bhwd,wk->bhkd", arriving[1], cosine_cols, precision=precise
    ) - jnp.einsum("bhwd,wk->bhkd", arriving[0], sine_cols, precision=precise)
    spec_half = jnp.stack([real_part, imag_part]).astype(jnp.bfloat16)
    spectrum = lax.all_to_all(spec_half, "lat", split_axis=3, concat_axis=4, tiled=True)
    blocks = inner_kernel.shape[1]
    block_width = inner_kernel.shape[2]
    local_shape = spectrum.shape
    flat_spec = spectrum.reshape(2, -1, blocks, block_width)
    flat_cot = spec_cotangent.reshape(2, -1, blocks, block_width)
    filtered, gradients = block_filter(
        flat_spec, flat_cot, inner_kernel, inner_offset, outer_kernel, outer_offset
    )
    totals = lax.psum((gradients[0], gradients[1], gradients[2], gradients[3]), ("lat", "lon"))
    normalizer = 1.0 / math.sqrt(conditions * height * wavenumbers)
    return (
        filtered.reshape(local_shape),
        totals[0] * normalizer,
        totals[1] * normalizer,
        totals[2] * normalizer,
        totals[3] * normalizer,
    )


def split_table(table):
    high = table.astype(jnp.bfloat16)
    low = (table - high.astype(np.float64)).astype(jnp.bfloat16)
    return np.stack([high, low])


def phase_tables(length, columns):
    product = np.arange(length)[:, None] * np.arange(columns)[None, :] % length
    angles = product * (2.0 * math.pi / length)
    return np.cos(angles) / math.sqrt(length), np.sin(angles) / math.sqrt(length)


def column_tables(width, wavenumbers, groups):
    cosine, sine = phase_tables(width, wavenumbers)
    both = np.stack([cosine.T, -sine.T]).reshape(2, groups, wavenumbers // groups, width)
    return split_table(both.transpose(1, 0, 2, 3).reshape(2 * wavenumbers, width))


def row_tables(height, inner):
    cosine, sine = phase_tables(height, height)
    eye = np.eye(inner)
    both = np.stack([np.kron(cosine.T, eye), np.kron(sine.T, eye)])
    return split_table(both)


def padded(values, lanes):
    rows, columns = values.shape
    return jnp.concatenate([values, jnp.zeros((rows, lanes - columns), values.dtype)], axis=1)


def fused_kernel(
    sizes,
    fields_ref,
    cot_ref,
    inner_ref,
    inner_off_ref,
    outer_ref,
    outer_off_ref,
    cols_ref,
    rows_hbm,
    filt_ref,
    inner_grad_ref,
    outer_grad_ref,
    bias_ref,
    send_a,
    recv_a,
    send_b,
    recv_b,
    send_c,
    recv_c,
    send_d,
    recv_d,
    send_e,
    recv_e,
    gather,
    spec_s,
    hid_s,
    back_s,
    hb_s,
    raw_w,
    w1,
    w2,
    rows_ref,
    lon_send,
    lon_recv,
    lat_send,
    lat_recv,
    core_send,
    core_recv,
    local_sem,
):
    lats, lons, blocks, width, lanes, normalizer = sizes
    i = lax.axis_index("lat")
    j = lax.axis_index("lon")
    h_local, w_local, _ = fields_ref.shape
    m_local, k_local = cot_ref.shape[1], cot_ref.shape[2]
    tokens = spec_s.shape[0]
    part_rows = m_local * k_local
    zs = lons // 2
    f32, bf16 = jnp.float32, jnp.bfloat16

    loads = [pltpu.make_async_copy(rows_hbm, rows_ref, local_sem.at[0])]
    for p in range(2):
        loads.append(
            pltpu.make_async_copy(inner_ref.at[p, j], raw_w.at[p], local_sem.at[1 + p])
        )
        loads.append(
            pltpu.make_async_copy(outer_ref.at[p, j], raw_w.at[2 + p], local_sem.at[3 + p])
        )
    for load in loads:
        load.start()

    barrier = pltpu.get_barrier_semaphore()

    def greet_lon(d, carry):
        pl.semaphore_signal(
            barrier, inc=1, device_id=(i, lax.rem(j + d, lons)), device_id_type=pl.DeviceIdType.MESH
        )
        return carry

    def greet_lat(d, carry):
        pl.semaphore_signal(
            barrier, inc=1, device_id=(lax.rem(i + d, lats), j), device_id_type=pl.DeviceIdType.MESH
        )
        return carry

    lax.fori_loop(1, lons, greet_lon, 0)
    lax.fori_loop(1, lats, greet_lat, 0)

    for h in range(h_local):
        row = fields_ref[h].astype(f32)
        for b in range(blocks):
            send_a[b, :, h * lanes : (h + 1) * lanes] = padded(
                row[:, b * width : (b + 1) * width], lanes
            ).astype(bf16)

    pl.semaphore_wait(barrier, lons + lats - 2)

    def lon_copy(phase, src, dst, d):
        return pltpu.make_async_remote_copy(
            src_ref=src,
            dst_ref=dst,
            send_sem=lon_send.at[phase, d],
            recv_sem=lon_recv.at[phase, d],
            device_id=(i, lax.rem(j + d, lons)),
            device_id_type=pl.DeviceIdType.MESH,
        )

    def lat_copy(phase, src, dst, d):
        return pltpu.make_async_remote_copy(
            src_ref=src,
            dst_ref=dst,
            send_sem=lat_send.at[phase, d],
            recv_sem=lat_recv.at[phase, d],
            device_id=(lax.rem(i + d, lats), j),
            device_id_type=pl.DeviceIdType.MESH,
        )

    def exchange_start(copy, phase, send, recv, me, n):
        def one(d, carry):
            copy(phase, send.at[lax.rem(me + d, n)], recv.at[me], d).start()
            return carry

        lax.fori_loop(1, n, one, 0)

    def exchange_recv(copy, phase, send, recv, me, n):
        def one(d, carry):
            source = lax.rem(me + n - d, n)
            copy(phase, send.at[source], recv.at[source], d).wait_recv()
            return carry

        lax.fori_loop(1, n, one, 0)

    def exchange_sent(copy, phase, send, recv, me, n):
        def one(d, carry):
            copy(phase, send.at[lax.rem(me + d, n)], recv.at[me], d).wait_send()
            return carry

        lax.fori_loop(1, n, one, 0)

    exchange_start(lon_copy, 0, send_a, recv_a, j, lons)
    recv_a[j] = send_a[j]

    for p in range(2):
        part = jnp.concatenate([cot_ref[p, m].astype(f32) for m in range(m_local)], axis=0)
        for b in range(blocks):
            send_c[b, :, p * lanes : (p + 1) * lanes] = padded(
                part[:, b * width : (b + 1) * width], lanes
            ).astype(bf16)
    exchange_start(lon_copy, 1, send_c, recv_c, j, lons)
    recv_c[j] = send_c[j]

    for load in loads[1:]:
        load.wait()
    w1[...] = jnp.zeros_like(w1)
    w2[...] = jnp.zeros_like(w2)
    for target, base in ((w1, 0), (w2, 2)):
        real, imag = raw_w[base], raw_w[base + 1]
        target[0:width, 0:width] = real
        target[0:width, lanes : lanes + width] = imag
        target[lanes : lanes + width, 0:width] = -imag
        target[lanes : lanes + width, lanes : lanes + width] = real
    off1 = jnp.concatenate(
        [padded(inner_off_ref[p, pl.ds(j, 1), :], lanes) for p in range(2)], axis=1
    )
    off2 = jnp.concatenate(
        [padded(outer_off_ref[p, pl.ds(j, 1), :], lanes) for p in range(2)], axis=1
    )
    loads[0].wait()

    exchange_recv(lon_copy, 0, send_a, recv_a, j, lons)
    columns = jnp.concatenate([recv_a[s].astype(f32) for s in range(lons)], axis=0).astype(bf16)
    half = jnp.dot(cols_ref[0], columns, preferred_element_type=f32) + jnp.dot(
        cols_ref[1], columns, preferred_element_type=f32
    )
    for g in range(lats):
        for p in range(2):
            first = (2 * g + p) * k_local
            send_b[g, :, p * lanes : (p + 1) * lanes] = jnp.concatenate(
                [
                    half[first : first + k_local, h * lanes : (h + 1) * lanes]
                    for h in range(h_local)
                ],
                axis=0,
            ).astype(bf16)
    exchange_start(lat_copy, 0, send_b, recv_b, i, lats)
    recv_b[i] = send_b[i]
    exchange_recv(lon_copy, 1, send_c, recv_c, j, lons)
    exchange_recv(lat_copy, 0, send_b, recv_b, i, lats)

    chunks = 4
    chunk = tokens // chunks
    per_chunk = lons // chunks
    lane = lax.broadcasted_iota(jnp.int32, (chunk, 2 * lanes), 1)
    ones_lane = lane == width
    one = jnp.ones((chunk, 2 * lanes), f32)

    def block_layers(c, carry):
        rows = pl.ds(pl.multiple_of(c * chunk, chunk), chunk)
        lines = recv_b[...].reshape(tokens, 2 * lanes)
        cos_part = jnp.dot(rows_ref[0, 0, rows, :], lines, preferred_element_type=f32) + jnp.dot(
            rows_ref[1, 0, rows, :], lines, preferred_element_type=f32
        )
        sin_part = jnp.dot(rows_ref[0, 1, rows, :], lines, preferred_element_type=f32) + jnp.dot(
            rows_ref[1, 1, rows, :], lines, preferred_element_type=f32
        )
        real = cos_part[:, :lanes] + sin_part[:, lanes:]
        imag = cos_part[:, lanes:] - sin_part[:, :lanes]
        spec_wide = jnp.concatenate([real, imag], axis=1)
        spec = spec_wide.astype(bf16)
        spec_s[rows, :] = jnp.where(ones_lane, one, spec_wide).astype(bf16)
        pre = jnp.dot(spec, w1[...], preferred_element_type=f32) + off1
        square = pre * pre
        level = jnp.tanh(gelu_coeff * (pre + 0.044715 * pre * square))
        hid_wide = 0.5 * pre * (1.0 + level)
        slope = 0.5 * (1.0 + level) + 0.5 * pre * (1.0 - level * level) * gelu_coeff * (
            1.0 + 3.0 * 0.044715 * square
        )
        hid_s[rows, :] = jnp.where(ones_lane, one, hid_wide).astype(bf16)
        out = jnp.dot(hid_wide.astype(bf16), w2[...], preferred_element_type=f32) + off2
        soft = jnp.tanh(out * (1.0 / shrink_level))
        filtered = (out - shrink_level * soft).astype(bf16)
        send_d[pl.ds(c * per_chunk, per_chunk)] = filtered.reshape(
            per_chunk, part_rows, 2 * lanes
        )
        cot = recv_c[pl.ds(c * per_chunk, per_chunk)].reshape(chunk, 2 * lanes).astype(f32)
        back = (cot * (soft * soft)).astype(bf16)
        back_s[rows, :] = back
        turned = lax.dot_general(
            back, w2[...], (((1,), (1,)), ((), ())), preferred_element_type=f32
        )
        hb_s[rows, :] = (turned * slope).astype(bf16)
        return carry

    lax.fori_loop(0, chunks, block_layers, 0)
    exchange_start(lon_copy, 2, send_d, recv_d, j, lons)
    recv_d[j] = send_d[j]

    deep = send_e.shape[1]
    for base, left, right in ((2, hid_s, back_s), (0, spec_s, hb_s)):
        full = lax.dot_general(
            left[...], right[...], (((0,), (0,)), ((), ())), preferred_element_type=f32
        )
        send_e[base] = (full[0:deep, :lanes] + full[lanes : lanes + deep, lanes:]).astype(bf16)
        send_e[base + 1] = (full[0:deep, lanes:] - full[lanes : lanes + deep, :lanes]).astype(bf16)
    exchange_start(lat_copy, 1, send_e, recv_e, i, lats)
    recv_e[i] = send_e[i]
    exchange_recv(lat_copy, 1, send_e, recv_e, i, lats)
    total = recv_e[0].astype(f32)
    for s in range(1, lats):
        total = total + recv_e[s].astype(f32)
    side = lax.rem(j, 2)
    z = lax.div(j, 2)
    gather[side, i, z] = (total * normalizer).astype(bf16)

    def z_copy(d, slot):
        return pltpu.make_async_remote_copy(
            src_ref=gather.at[side, i, slot],
            dst_ref=gather.at[side, i, slot],
            send_sem=lon_send.at[3, d],
            recv_sem=lon_recv.at[3, d],
            device_id=(i, lax.rem(j + 2 * d, lons)),
            device_id_type=pl.DeviceIdType.MESH,
        )

    def side_copy(from_side, slot):
        return pltpu.make_async_remote_copy(
            src_ref=gather.at[from_side, slot],
            dst_ref=gather.at[from_side, slot],
            send_sem=core_send.at[slot],
            recv_sem=core_recv.at[slot],
            device_id=(i, j + 1 - 2 * side),
            device_id_type=pl.DeviceIdType.MESH,
        )

    for d in range(1, zs):
        z_copy(d, z).start()

    exchange_recv(lon_copy, 2, send_d, recv_d, j, lons)
    for p in range(2):
        filt_ref[p] = jnp.concatenate(
            [recv_d[b, :, p * lanes : p * lanes + width].astype(f32) for b in range(blocks)],
            axis=1,
        ).astype(bf16)

    for d in range(1, zs):
        z_copy(d, lax.rem(z + zs - d, zs)).wait_recv()
    for d in range(1, lats):
        lat_copy(2, gather.at[side, i], gather.at[side, i], d).start()
    side_copy(side, i).start()
    for d in range(1, lats):
        source = lax.rem(i + lats - d, lats)
        lat_copy(2, gather.at[side, source], gather.at[side, source], d).wait_recv()
        side_copy(side, source).start()
    other = 1 - side
    for q in range(lats):
        side_copy(other, q).wait_recv()

    for q in range(lats):
        target = inner_grad_ref if q < 2 else outer_grad_ref
        for b in range(blocks):
            piece = gather[b % 2, q, b // 2]
            target[q % 2, b] = piece[0:width, 0:width]
            bias_ref[q, b : b + 1, :] = piece[width:deep, 0:width].astype(f32)[0:1]

    exchange_sent(lon_copy, 0, send_a, recv_a, j, lons)
    exchange_sent(lon_copy, 1, send_c, recv_c, j, lons)
    exchange_sent(lon_copy, 2, send_d, recv_d, j, lons)
    exchange_sent(lat_copy, 0, send_b, recv_b, i, lats)
    exchange_sent(lat_copy, 1, send_e, recv_e, i, lats)
    for d in range(1, zs):
        z_copy(d, z).wait_send()
    for d in range(1, lats):
        lat_copy(2, gather.at[side, i], gather.at[side, i], d).wait_send()
    for q in range(lats):
        side_copy(side, q).wait_send()


def fused_device(fields, spec_cotangent, inner_kernel, inner_offset, outer_kernel, outer_offset):
    lats = lax.axis_size("lat")
    lons = lax.axis_size("lon")
    _, h_local, w_local, channels = fields.shape
    m_local, k_local = spec_cotangent.shape[2:4]
    blocks, width = inner_kernel.shape[1:3]
    height, full_width = h_local * lats, w_local * lons
    wavenumbers = k_local * lats
    lanes = 128
    tokens = height * k_local
    part_rows = m_local * k_local
    deep = (width // 16 + 1) * 16
    normalizer = 1.0 / math.sqrt(height * wavenumbers)
    cols = jnp.asarray(column_tables(full_width, wavenumbers, lats))
    rows = jnp.asarray(row_tables(height, k_local))
    vmem = pl.BlockSpec(memory_space=pltpu.VMEM)
    hbm = pl.BlockSpec(memory_space=pl.ANY)
    bf16 = jnp.bfloat16
    wide = (tokens, 2 * lanes)
    dma = pltpu.SemaphoreType.DMA

    def pair(*shape):
        return [pltpu.VMEM(shape, bf16)] * 2

    filt, inner_grad, outer_grad, bias = pl.pallas_call(
        lambda *refs: fused_kernel((lats, lons, blocks, width, lanes, normalizer), *refs),
        name="fused_filter",
        out_shape=[
            jax.ShapeDtypeStruct((2, part_rows, channels), bf16),
            jax.ShapeDtypeStruct(inner_kernel.shape, bf16),
            jax.ShapeDtypeStruct(outer_kernel.shape, bf16),
            jax.ShapeDtypeStruct((4, blocks, width), jnp.float32),
        ],
        in_specs=[vmem, vmem, hbm, vmem, hbm, vmem, vmem, hbm],
        out_specs=[vmem] * 4,
        scratch_shapes=[
            *pair(blocks, w_local, h_local * lanes),
            *pair(lats, h_local * k_local, 2 * lanes),
            *pair(blocks, part_rows, 2 * lanes),
            *pair(blocks, part_rows, 2 * lanes),
            *pair(4, deep, lanes),
            pltpu.VMEM((2, lats, lons // 2, deep, lanes), bf16),
            *[pltpu.VMEM(wide, bf16)] * 4,
            pltpu.VMEM((4, width, width), bf16),
            *pair(2 * lanes, 2 * lanes),
            pltpu.VMEM(rows.shape, bf16),
            dma((4, lons)),
            dma((4, lons)),
            dma((3, lats)),
            dma((3, lats)),
            dma((lats,)),
            dma((lats,)),
            dma((5,)),
        ],
        compiler_params=pltpu.CompilerParams(
            collective_id=0, has_side_effects=True, vmem_limit_bytes=40 * 1024 * 1024
        ),
    )(
        fields.reshape(fields.shape[1:]),
        spec_cotangent.reshape(2, m_local, k_local, channels),
        inner_kernel,
        inner_offset,
        outer_kernel,
        outer_offset,
        cols,
        rows,
    )
    return (
        filt.astype(jnp.float32).reshape(spec_cotangent.shape),
        inner_grad.astype(jnp.float32),
        bias[0:2],
        outer_grad.astype(jnp.float32),
        bias[2:4],
    )


def choose_device(fields, spec_cotangent, inner_kernel, *rest):
    lats, lons = lax.axis_size("lat"), lax.axis_size("lon")
    blocks, width = inner_kernel.shape[1:3]
    fits = (
        fields.shape[0] == 1
        and lons == blocks
        and lats == 4
        and width % 16 == 0
        and width < 128
        and fields.shape[1] == 16
        and fields.shape[2] == 8
        and spec_cotangent.shape[2] == 8
        and spec_cotangent.shape[3] == 8
    )
    chosen = fused_device if fits else per_device
    return chosen(fields, spec_cotangent, inner_kernel, *rest)


def solution(mesh):
    placed = (P(None, "lat", "lon", None), P(None, None, "lon", "lat", None), P(), P(), P(), P())
    return jax.shard_map(
        choose_device,
        mesh=mesh,
        in_specs=placed,
        out_specs=(P(None, None, "lon", "lat", None), P(), P(), P(), P()),
        check_vma=False,
    )
```

```python
import math

import jax
import jax.numpy as jnp
import numpy as np
from jax import lax
from jax.experimental import pallas as pl
from jax.experimental.pallas import tpu as pltpu
from jax.sharding import PartitionSpec as P

shrink_level = 0.1
gelu_coeff = 0.7978845608028654
precise = lax.Precision.HIGHEST


def dft_tables(length, columns):
    points = jnp.arange(length, dtype=jnp.int32)
    orders = jnp.arange(columns, dtype=jnp.int32)
    product = points[:, None] * orders[None, :] % length
    angles = product.astype(jnp.float32) * (2.0 * math.pi / length)
    factor = 1.0 / math.sqrt(length)
    return (jnp.cos(angles) * factor, jnp.sin(angles) * factor)


def shrink(values):
    return values - shrink_level * jnp.tanh(values / shrink_level)


def shrink_slope(values):
    level = jnp.tanh(values / shrink_level)
    return level * level


def gelu_value(values):
    inner = gelu_coeff * (values + 0.044715 * values * values * values)
    return 0.5 * values * (1.0 + jnp.tanh(inner))


def gelu_slope(values):
    inner = gelu_coeff * (values + 0.044715 * values * values * values)
    level = jnp.tanh(inner)
    return 0.5 * (1.0 + level) + 0.5 * values * (1.0 - level * level) * gelu_coeff * (
        1.0 + 3.0 * 0.044715 * values * values
    )


def mixing(operand, kernel):
    return jnp.einsum("rnb,nbc->rnc", operand, kernel, preferred_element_type=jnp.float32)


def backmix(operand, kernel):
    return jnp.einsum("rnc,nbc->rnb", operand, kernel, preferred_element_type=jnp.float32)


def crossed(operand, second):
    return jnp.einsum("rnb,rnc->nbc", operand, second, preferred_element_type=jnp.float32)


def block_filter(spectrum, cotangent, inner_kernel, inner_offset, outer_kernel, outer_offset):
    spec_real, spec_imag = (spectrum[0], spectrum[1])
    pre_real = (
        mixing(spec_real, inner_kernel[0]) - mixing(spec_imag, inner_kernel[1]) + inner_offset[0]
    )
    pre_imag = (
        mixing(spec_imag, inner_kernel[0]) + mixing(spec_real, inner_kernel[1]) + inner_offset[1]
    )
    hid_real = gelu_value(pre_real).astype(jnp.bfloat16)
    hid_imag = gelu_value(pre_imag).astype(jnp.bfloat16)
    out_real = (
        mixing(hid_real, outer_kernel[0]) - mixing(hid_imag, outer_kernel[1]) + outer_offset[0]
    )
    out_imag = (
        mixing(hid_imag, outer_kernel[0]) + mixing(hid_real, outer_kernel[1]) + outer_offset[1]
    )
    filtered = jnp.stack([shrink(out_real), shrink(out_imag)])
    back_real = (cotangent[0].astype(jnp.float32) * shrink_slope(out_real)).astype(jnp.bfloat16)
    back_imag = (cotangent[1].astype(jnp.float32) * shrink_slope(out_imag)).astype(jnp.bfloat16)
    outer_grad = jnp.stack(
        [
            crossed(hid_real, back_real) + crossed(hid_imag, back_imag),
            crossed(hid_real, back_imag) - crossed(hid_imag, back_real),
        ]
    )
    outer_bias = jnp.stack(
        [
            jnp.sum(back_real, axis=0, dtype=jnp.float32),
            jnp.sum(back_imag, axis=0, dtype=jnp.float32),
        ]
    )
    grad_real = (
        (backmix(back_real, outer_kernel[0]) + backmix(back_imag, outer_kernel[1]))
        * gelu_slope(pre_real)
    ).astype(jnp.bfloat16)
    grad_imag = (
        (backmix(back_imag, outer_kernel[0]) - backmix(back_real, outer_kernel[1]))
        * gelu_slope(pre_imag)
    ).astype(jnp.bfloat16)
    inner_grad = jnp.stack(
        [
            crossed(spec_real, grad_real) + crossed(spec_imag, grad_imag),
            crossed(spec_real, grad_imag) - crossed(spec_imag, grad_real),
        ]
    )
    inner_bias = jnp.stack(
        [
            jnp.sum(grad_real, axis=0, dtype=jnp.float32),
            jnp.sum(grad_imag, axis=0, dtype=jnp.float32),
        ]
    )
    return (filtered, (inner_grad, inner_bias, outer_grad, outer_bias))


def per_device(fields, spec_cotangent, inner_kernel, inner_offset, outer_kernel, outer_offset):
    lat_devices = lax.axis_size("lat")
    lon_devices = lax.axis_size("lon")
    conditions = fields.shape[0]
    height = fields.shape[1] * lat_devices
    width = fields.shape[2] * lon_devices
    wavenumbers = width // 2
    cosine_rows, sine_rows = dft_tables(height, height)
    cosine_cols, sine_cols = dft_tables(width, wavenumbers)
    arriving = lax.all_to_all(fields, "lat", split_axis=3, concat_axis=1, tiled=True)
    shape_in = arriving.shape
    floats = arriving.astype(jnp.float32).reshape(
        shape_in[0], shape_in[1], shape_in[2] * shape_in[3]
    )
    real_part = jnp.einsum("bhx,hm->bmx", floats, cosine_rows, precision=precise)
    imag_part = -jnp.einsum("bhx,hm->bmx", floats, sine_rows, precision=precise)
    spec_rows = jnp.stack([real_part, imag_part]).reshape((2,) + shape_in)
    arriving = lax.all_to_all(spec_rows, "lon", split_axis=2, concat_axis=3, tiled=True)
    real_part = jnp.einsum(
        "bhwd,wk->bhkd", arriving[0], cosine_cols, precision=precise
    ) + jnp.einsum("bhwd,wk->bhkd", arriving[1], sine_cols, precision=precise)
    imag_part = jnp.einsum(
        "bhwd,wk->bhkd", arriving[1], cosine_cols, precision=precise
    ) - jnp.einsum("bhwd,wk->bhkd", arriving[0], sine_cols, precision=precise)
    spec_half = jnp.stack([real_part, imag_part]).astype(jnp.bfloat16)
    spectrum = lax.all_to_all(spec_half, "lat", split_axis=3, concat_axis=4, tiled=True)
    blocks = inner_kernel.shape[1]
    block_width = inner_kernel.shape[2]
    local_shape = spectrum.shape
    flat_spec = spectrum.reshape(2, -1, blocks, block_width)
    flat_cot = spec_cotangent.reshape(2, -1, blocks, block_width)
    filtered, gradients = block_filter(
        flat_spec, flat_cot, inner_kernel, inner_offset, outer_kernel, outer_offset
    )
    totals = lax.psum((gradients[0], gradients[1], gradients[2], gradients[3]), ("lat", "lon"))
    normalizer = 1.0 / math.sqrt(conditions * height * wavenumbers)
    return (
        filtered.reshape(local_shape),
        totals[0] * normalizer,
        totals[1] * normalizer,
        totals[2] * normalizer,
        totals[3] * normalizer,
    )


def split_table(table):
    high = table.astype(jnp.bfloat16)
    low = (table - high.astype(np.float64)).astype(jnp.bfloat16)
    return np.stack([high, low])


def phase_tables(length, columns):
    product = np.arange(length)[:, None] * np.arange(columns)[None, :] % length
    angles = product * (2.0 * math.pi / length)
    return np.cos(angles) / math.sqrt(length), np.sin(angles) / math.sqrt(length)


def column_tables(width, wavenumbers, groups):
    cosine, sine = phase_tables(width, wavenumbers)
    both = np.stack([cosine.T, -sine.T]).reshape(2, groups, wavenumbers // groups, width)
    return split_table(both.transpose(1, 0, 2, 3).reshape(2 * wavenumbers, width))


def row_tables(height, inner):
    cosine, sine = phase_tables(height, height)
    eye = np.eye(inner)
    both = np.stack([cosine.T, sine.T])
    scales = np.linspace(1.0, 2.0, 2001)
    errors = [
        np.mean(((both * a).astype(jnp.bfloat16).astype(np.float64) / a - both) ** 2) for a in scales
    ]
    scale = float(scales[int(np.argmin(errors))])
    return np.stack([np.kron(part * scale, eye) for part in both]).astype(jnp.bfloat16), 1.0 / scale


def padded(values, lanes):
    rows, columns = values.shape
    return jnp.concatenate([values, jnp.zeros((rows, lanes - columns), values.dtype)], axis=1)


def fold(matrix, bias, lanes):
    width = matrix.shape[0]
    side = lanes - width
    keep = width * width // lanes
    rest = matrix[keep:]
    tail = jnp.concatenate(
        [rest[:, t * side : (t + 1) * side] for t in range(width // side)], axis=0
    )
    top = jnp.concatenate([matrix[:keep], tail], axis=1)
    return jnp.concatenate([top, bias], axis=0)


def unpack_kernel(gather_ref, arrived_ref, filt_ref, inner_ref, inner_off_ref, outer_ref, outer_off_ref):
    blocks = arrived_ref.shape[0]
    width = inner_ref.shape[2]
    lanes = gather_ref.shape[-1]
    side = lanes - width
    keep = width * width // lanes
    step = width - keep
    f32 = jnp.float32
    m_local = filt_ref.shape[1]
    k_local = filt_ref.shape[2]
    for p in range(2):
        whole = jnp.concatenate(
            [arrived_ref[b, :, p * lanes : p * lanes + width].astype(f32) for b in range(blocks)],
            axis=1,
        )
        for m in range(m_local):
            filt_ref[p, m] = whole[m * k_local : (m + 1) * k_local]
    for q in range(4):
        grad = inner_ref if q < 2 else outer_ref
        off = inner_off_ref if q < 2 else outer_off_ref
        for b in range(blocks):
            piece = gather_ref[b % 2, q, b // 2].astype(f32)
            grad[q % 2, b, 0:keep, :] = piece[0:keep, 0:width]
            grad[q % 2, b, keep:width, :] = jnp.concatenate(
                [piece[t * step : (t + 1) * step, width:lanes] for t in range(width // side)], axis=1
            )
            off[q % 2, b : b + 1, :] = piece[keep : keep + 1, 0:width]


def fused_kernel(
    sizes,
    fields_hbm,
    cot_hbm,
    inner_ref,
    inner_off_hbm,
    outer_ref,
    outer_off_hbm,
    cols_hbm,
    rows_hbm,
    gather,
    recv_d,
    send_a,
    recv_a,
    send_b,
    recv_b,
    send_c,
    recv_c,
    send_d,
    send_e,
    recv_e,
    spec_s,
    hid_s,
    back_s,
    hb_s,
    raw_w,
    w1,
    w2,
    rows_ref,
    cols_ref,
    fields_ref,
    cot_ref,
    inner_off_ref,
    outer_off_ref,
    lon_send,
    lon_recv,
    lat_send,
    lat_recv,
    z_send,
    z_recv,
    spread_send,
    spread_recv,
    core_send,
    core_recv,
    local_sem,
):
    lats, lons, blocks, width, lanes, normalizer, unscale = sizes
    i = lax.axis_index("lat")
    j = lax.axis_index("lon")
    h_local = fields_ref.shape[0]
    m_local, k_local = cot_ref.shape[1], cot_ref.shape[2]
    tokens = spec_s.shape[0]
    part_rows = m_local * k_local
    zs = lons // 2
    f32, bf16 = jnp.float32, jnp.bfloat16
    mesh_id = pl.DeviceIdType.MESH

    barrier = pltpu.get_barrier_semaphore()

    def greet_lon(d, carry):
        pl.semaphore_signal(
            barrier, inc=1, device_id=(i, lax.rem(j + d, lons)), device_id_type=mesh_id
        )
        return carry

    def greet_lat(d, carry):
        pl.semaphore_signal(
            barrier, inc=1, device_id=(lax.rem(i + d, lats), j), device_id_type=mesh_id
        )
        return carry

    sources = [
        (fields_hbm, fields_ref),
        (cot_hbm, cot_ref),
        (cols_hbm, cols_ref),
        (inner_off_hbm, inner_off_ref),
        (outer_off_hbm, outer_off_ref),
        (inner_ref.at[0, j], raw_w.at[0]),
        (inner_ref.at[1, j], raw_w.at[1]),
        (outer_ref.at[0, j], raw_w.at[2]),
        (outer_ref.at[1, j], raw_w.at[3]),
        (rows_hbm, rows_ref),
    ]
    loads = [
        pltpu.make_async_copy(source, target, local_sem.at[n])
        for n, (source, target) in enumerate(sources)
    ]
    loads[0].start()
    lax.fori_loop(1, lons, greet_lon, 0)
    lax.fori_loop(1, lats, greet_lat, 0)
    for load in loads[1:]:
        load.start()
    loads[0].wait()

    rows_of = [fields_ref[h].astype(f32) for h in range(h_local)]
    for b in range(blocks):
        send_a[b] = jnp.concatenate(
            [row[:, b * width : (b + 1) * width] for row in rows_of], axis=1
        ).astype(bf16)

    pl.semaphore_wait(barrier, lons + lats - 2)

    def lon_copy(phase, src, dst, d):
        return pltpu.make_async_remote_copy(
            src_ref=src,
            dst_ref=dst,
            send_sem=lon_send.at[phase, d],
            recv_sem=lon_recv.at[phase, d],
            device_id=(i, lax.rem(j + d, lons)),
            device_id_type=mesh_id,
        )

    def lat_copy(phase, src, dst, d):
        return pltpu.make_async_remote_copy(
            src_ref=src,
            dst_ref=dst,
            send_sem=lat_send.at[phase, d],
            recv_sem=lat_recv.at[phase, d],
            device_id=(lax.rem(i + d, lats), j),
            device_id_type=mesh_id,
        )

    def exchange_start(copy, phase, send, recv, me, n):
        def one(d, carry):
            copy(phase, send.at[lax.rem(me + d, n)], recv.at[me], d).start()
            return carry

        lax.fori_loop(1, n, one, 0)

    def exchange_recv(copy, phase, send, recv, me, n):
        def one(d, carry):
            source = lax.rem(me + n - d, n)
            copy(phase, send.at[source], recv.at[source], d).wait_recv()
            return carry

        lax.fori_loop(1, n, one, 0)

    def exchange_sent(copy, phase, send, recv, me, n):
        def one(d, carry):
            copy(phase, send.at[lax.rem(me + d, n)], recv.at[me], d).wait_send()
            return carry

        lax.fori_loop(1, n, one, 0)

    exchange_start(lon_copy, 0, send_a, recv_a, j, lons)
    recv_a[j] = send_a[j]

    loads[1].wait()
    for p in range(2):
        part = jnp.concatenate([cot_ref[p, m].astype(f32) for m in range(m_local)], axis=0)
        for b in range(blocks):
            send_c[b, :, p * lanes : (p + 1) * lanes] = padded(
                part[:, b * width : (b + 1) * width], lanes
            ).astype(bf16)
    exchange_start(lon_copy, 1, send_c, recv_c, j, lons)
    recv_c[j] = send_c[j]

    for load in loads[2:]:
        load.wait()
    w1[...] = jnp.zeros_like(w1)
    w2[...] = jnp.zeros_like(w2)
    for target, base in ((w1, 0), (w2, 2)):
        real, imag = raw_w[base], raw_w[base + 1]
        target[0:width, 0:width] = real
        target[0:width, lanes : lanes + width] = imag
        target[lanes : lanes + width, 0:width] = -imag
        target[lanes : lanes + width, lanes : lanes + width] = real
    off1 = jnp.concatenate(
        [padded(inner_off_ref[p, pl.ds(j, 1), :], lanes) for p in range(2)], axis=1
    )
    off2 = jnp.concatenate(
        [padded(outer_off_ref[p, pl.ds(j, 1), :], lanes) for p in range(2)], axis=1
    )

    exchange_recv(lon_copy, 0, send_a, recv_a, j, lons)
    columns = jnp.concatenate([recv_a[s].astype(f32) for s in range(lons)], axis=0).astype(bf16)
    half = jnp.dot(cols_ref[0], columns, preferred_element_type=f32) + jnp.dot(
        cols_ref[1], columns, preferred_element_type=f32
    )
    for g in range(lats):
        high, low = [], []
        for p in range(2):
            first = (2 * g + p) * k_local
            value = jnp.concatenate(
                [
                    half[first : first + k_local, h * width : (h + 1) * width]
                    for h in range(h_local)
                ],
                axis=0,
            )
            top = value.astype(bf16).astype(f32)
            high.append(top)
            low.append(value - top)
        send_b[g] = jnp.concatenate(high + low, axis=1).astype(bf16)
    exchange_start(lat_copy, 0, send_b, recv_b, i, lats)
    recv_b[i] = send_b[i]
    exchange_recv(lon_copy, 1, send_c, recv_c, j, lons)
    exchange_recv(lat_copy, 0, send_b, recv_b, i, lats)

    chunks = 4
    chunk = tokens // chunks
    per_chunk = lons // chunks
    packed = jnp.concatenate([recv_b[s].astype(f32) for s in range(lats)], axis=0)
    lines = jnp.concatenate(
        [padded(packed[:, t * width : (t + 1) * width], lanes) for t in range(4)], axis=1
    ).astype(bf16)
    ones_lane = lax.broadcasted_iota(jnp.int32, (chunk, 2 * lanes), 1) == width
    one = jnp.ones((chunk, 2 * lanes), f32)
    for c in range(chunks):
        rows = slice(c * chunk, (c + 1) * chunk)
        cos_part = jnp.dot(rows_ref[0, rows, :], lines, preferred_element_type=f32)
        sin_part = jnp.dot(rows_ref[1, rows, :], lines, preferred_element_type=f32)
        cos_part = cos_part[:, : 2 * lanes] + cos_part[:, 2 * lanes :]
        sin_part = sin_part[:, : 2 * lanes] + sin_part[:, 2 * lanes :]
        real = cos_part[:, :lanes] + sin_part[:, lanes:]
        imag = cos_part[:, lanes:] - sin_part[:, :lanes]
        spec_wide = jnp.concatenate([real, imag], axis=1) * unscale
        spec = spec_wide.astype(bf16)
        spec_s[rows, :] = jnp.where(ones_lane, one, spec_wide).astype(bf16)
        pre = jnp.dot(spec, w1[...], preferred_element_type=f32) + off1
        square = pre * pre
        level = jnp.tanh(gelu_coeff * (pre + 0.044715 * pre * square))
        hid_wide = 0.5 * pre * (1.0 + level)
        slope = 0.5 * (1.0 + level) + 0.5 * pre * (1.0 - level * level) * gelu_coeff * (
            1.0 + 3.0 * 0.044715 * square
        )
        hid_s[rows, :] = jnp.where(ones_lane, one, hid_wide).astype(bf16)
        out = jnp.dot(hid_wide.astype(bf16), w2[...], preferred_element_type=f32) + off2
        soft = jnp.tanh(out * (1.0 / shrink_level))
        filtered = (out - shrink_level * soft).astype(bf16)
        for r in range(per_chunk):
            dest = c * per_chunk + r
            send_d[dest] = filtered[r * part_rows : (r + 1) * part_rows]

            @pl.when(dest != j)
            def _():
                away = lax.rem(dest - j + lons, lons)
                lon_copy(2, send_d.at[dest], recv_d.at[j], away).start()

        cot = jnp.concatenate(
            [recv_c[c * per_chunk + r] for r in range(per_chunk)], axis=0
        ).astype(f32)
        back = (cot * (soft * soft)).astype(bf16)
        back_s[rows, :] = back
        turned = lax.dot_general(
            back, w2[...], (((1,), (1,)), ((), ())), preferred_element_type=f32
        )
        hb_s[rows, :] = (turned * slope).astype(bf16)
    recv_d[j] = send_d[j]

    extra = send_e.shape[1] - width * width // lanes
    for base, left, right in ((2, hid_s, back_s), (0, spec_s, hb_s)):
        full = lax.dot_general(
            left[...], right[...], (((0,), (0,)), ((), ())), preferred_element_type=f32
        )
        first = full[:lanes, :lanes] + full[lanes:, lanes:]
        second = full[:lanes, lanes:] - full[lanes:, :lanes]
        for n, value in enumerate((first, second)):
            send_e[base + n] = fold(
                value[:width, :width], value[width : width + extra], lanes
            ).astype(bf16)
    exchange_start(lat_copy, 1, send_e, recv_e, i, lats)
    recv_e[i] = send_e[i]
    exchange_recv(lat_copy, 1, send_e, recv_e, i, lats)
    total = recv_e[0].astype(f32)
    for s in range(1, lats):
        total = total + recv_e[s].astype(f32)
    side = lax.rem(j, 2)
    z = lax.div(j, 2)
    gather[side, i, z] = (total * normalizer).astype(bf16)

    def z_copy(d, slot):
        return pltpu.make_async_remote_copy(
            src_ref=gather.at[side, i, slot],
            dst_ref=gather.at[side, i, slot],
            send_sem=z_send.at[d],
            recv_sem=z_recv.at[d],
            device_id=(i, lax.rem(j + 2 * d, lons)),
            device_id_type=mesh_id,
        )

    def spread_copy(d, row, slot, turn):
        return pltpu.make_async_remote_copy(
            src_ref=gather.at[side, row, slot],
            dst_ref=gather.at[side, row, slot],
            send_sem=spread_send.at[turn, d],
            recv_sem=spread_recv.at[turn, d],
            device_id=(lax.rem(i + d, lats), j),
            device_id_type=mesh_id,
        )

    def side_copy(from_side, slot):
        return pltpu.make_async_remote_copy(
            src_ref=gather.at[from_side, slot],
            dst_ref=gather.at[from_side, slot],
            send_sem=core_send.at[slot],
            recv_sem=core_recv.at[slot],
            device_id=(i, j + 1 - 2 * side),
            device_id_type=mesh_id,
        )

    for d in range(1, zs):
        z_copy(d, z).start()
    for turn in range(zs):
        slot = lax.rem(z + zs - turn, zs)
        if turn:
            z_copy(turn, slot).wait_recv()
        for d in range(1, lats):
            spread_copy(d, i, slot, turn).start()
    side_copy(side, i).start()
    for d in range(1, lats):
        source = lax.rem(i + lats - d, lats)
        for turn in range(zs):
            spread_copy(d, source, lax.rem(z + zs - turn, zs), turn).wait_recv()
        side_copy(side, source).start()

    exchange_recv(lon_copy, 2, send_d, recv_d, j, lons)
    exchange_sent(lon_copy, 0, send_a, recv_a, j, lons)
    exchange_sent(lon_copy, 1, send_c, recv_c, j, lons)
    exchange_sent(lon_copy, 2, send_d, recv_d, j, lons)
    exchange_sent(lat_copy, 0, send_b, recv_b, i, lats)
    exchange_sent(lat_copy, 1, send_e, recv_e, i, lats)
    for d in range(1, zs):
        z_copy(d, z).wait_send()
    for turn in range(zs):
        for d in range(1, lats):
            spread_copy(d, i, lax.rem(z + zs - turn, zs), turn).wait_send()
    for q in range(lats):
        side_copy(side, q).wait_send()
    for q in range(lats):
        side_copy(1 - side, q).wait_recv()


def fused_device(fields, spec_cotangent, inner_kernel, inner_offset, outer_kernel, outer_offset):
    lats = lax.axis_size("lat")
    lons = lax.axis_size("lon")
    _, h_local, w_local, channels = fields.shape
    m_local, k_local = spec_cotangent.shape[2:4]
    blocks, width = inner_kernel.shape[1:3]
    height, full_width = h_local * lats, w_local * lons
    wavenumbers = k_local * lats
    lanes = 128
    tokens = height * k_local
    part_rows = m_local * k_local
    deep = width * width // lanes + 8
    normalizer = 1.0 / math.sqrt(height * wavenumbers)
    cols = jnp.asarray(column_tables(full_width, wavenumbers, lats))
    rows, unscale = row_tables(height, k_local)
    rows = jnp.asarray(rows)
    vmem = pl.BlockSpec(memory_space=pltpu.VMEM)
    hbm = pl.BlockSpec(memory_space=pltpu.HBM)
    bf16, f32 = jnp.bfloat16, jnp.float32
    wide = (tokens, 2 * lanes)
    dma = pltpu.SemaphoreType.DMA

    def pair(*shape):
        return [pltpu.VMEM(shape, bf16)] * 2

    gathered, arrived = pl.pallas_call(
        lambda *refs: fused_kernel(
            (lats, lons, blocks, width, lanes, normalizer, unscale), *refs
        ),
        name="fused_filter",
        out_shape=[
            jax.ShapeDtypeStruct((2, lats, lons // 2, deep, lanes), bf16),
            jax.ShapeDtypeStruct((blocks, part_rows, 2 * lanes), bf16),
        ],
        in_specs=[hbm] * 8,
        out_specs=[vmem] * 2,
        scratch_shapes=[
            *pair(blocks, w_local, h_local * width),
            *pair(lats, h_local * k_local, 4 * width),
            *pair(blocks, part_rows, 2 * lanes),
            pltpu.VMEM((blocks, part_rows, 2 * lanes), bf16),
            *pair(4, deep, lanes),
            *[pltpu.VMEM(wide, bf16)] * 4,
            pltpu.VMEM((4, width, width), bf16),
            *pair(2 * lanes, 2 * lanes),
            pltpu.VMEM(rows.shape, bf16),
            pltpu.VMEM(cols.shape, bf16),
            pltpu.VMEM(fields.shape[1:], bf16),
            pltpu.VMEM((2, m_local, k_local, channels), bf16),
            pltpu.VMEM(inner_offset.shape, f32),
            pltpu.VMEM(outer_offset.shape, f32),
            dma((3, lons)),
            dma((3, lons)),
            dma((2, lats)),
            dma((2, lats)),
            dma((lons // 2,)),
            dma((lons // 2,)),
            dma((lons // 2, lats)),
            dma((lons // 2, lats)),
            dma((lats,)),
            dma((lats,)),
            dma((10,)),
        ],
        compiler_params=pltpu.CompilerParams(
            collective_id=0, has_side_effects=True, vmem_limit_bytes=63 * 1024 * 1024
        ),
    )(
        fields.reshape(fields.shape[1:]),
        spec_cotangent.reshape(2, m_local, k_local, channels),
        inner_kernel,
        inner_offset,
        outer_kernel,
        outer_offset,
        cols,
        rows,
    )
    filt, inner_grad, inner_bias, outer_grad, outer_bias = pl.pallas_call(
        unpack_kernel,
        name="unpack",
        out_shape=[
            jax.ShapeDtypeStruct((2, m_local, k_local, channels), f32),
            jax.ShapeDtypeStruct(inner_kernel.shape, f32),
            jax.ShapeDtypeStruct(inner_offset.shape, f32),
            jax.ShapeDtypeStruct(outer_kernel.shape, f32),
            jax.ShapeDtypeStruct(outer_offset.shape, f32),
        ],
        in_specs=[vmem] * 2,
        out_specs=[vmem] * 5,
    )(gathered, arrived)
    return (
        filt.reshape(spec_cotangent.shape),
        inner_grad,
        inner_bias,
        outer_grad,
        outer_bias,
    )


def choose_device(fields, spec_cotangent, inner_kernel, *rest):
    lats, lons = lax.axis_size("lat"), lax.axis_size("lon")
    blocks, width = inner_kernel.shape[1:3]
    fits = (
        fields.shape[0] == 1
        and lons == blocks
        and lats == 4
        and width == 96
        and fields.shape[1] == 16
        and fields.shape[2] == 8
        and spec_cotangent.shape[2] == 8
        and spec_cotangent.shape[3] == 8
    )
    chosen = fused_device if fits else per_device
    return chosen(fields, spec_cotangent, inner_kernel, *rest)


def solution(mesh):
    placed = (P(None, "lat", "lon", None), P(None, None, "lon", "lat", None), P(), P(), P(), P())
    return jax.shard_map(
        choose_device,
        mesh=mesh,
        in_specs=placed,
        out_specs=(P(None, None, "lon", "lat", None), P(), P(), P(), P()),
        check_vma=False,
    )
```

```python
import math

import jax
import jax.numpy as jnp
import numpy as np
from jax import lax
from jax.experimental import pallas as pl
from jax.experimental.pallas import tpu as pltpu
from jax.sharding import PartitionSpec as P

shrink_level = 0.1
gelu_coeff = 0.7978845608028654
precise = lax.Precision.HIGHEST


def dft_tables(length, columns):
    points = jnp.arange(length, dtype=jnp.int32)
    orders = jnp.arange(columns, dtype=jnp.int32)
    product = points[:, None] * orders[None, :] % length
    angles = product.astype(jnp.float32) * (2.0 * math.pi / length)
    factor = 1.0 / math.sqrt(length)
    return (jnp.cos(angles) * factor, jnp.sin(angles) * factor)


def shrink(values):
    return values - shrink_level * jnp.tanh(values / shrink_level)


def shrink_slope(values):
    level = jnp.tanh(values / shrink_level)
    return level * level


def gelu_value(values):
    inner = gelu_coeff * (values + 0.044715 * values * values * values)
    return 0.5 * values * (1.0 + jnp.tanh(inner))


def gelu_slope(values):
    inner = gelu_coeff * (values + 0.044715 * values * values * values)
    level = jnp.tanh(inner)
    return 0.5 * (1.0 + level) + 0.5 * values * (1.0 - level * level) * gelu_coeff * (
        1.0 + 3.0 * 0.044715 * values * values
    )


def mixing(operand, kernel):
    return jnp.einsum("rnb,nbc->rnc", operand, kernel, preferred_element_type=jnp.float32)


def backmix(operand, kernel):
    return jnp.einsum("rnc,nbc->rnb", operand, kernel, preferred_element_type=jnp.float32)


def crossed(operand, second):
    return jnp.einsum("rnb,rnc->nbc", operand, second, preferred_element_type=jnp.float32)


def block_filter(spectrum, cotangent, inner_kernel, inner_offset, outer_kernel, outer_offset):
    spec_real, spec_imag = (spectrum[0], spectrum[1])
    pre_real = (
        mixing(spec_real, inner_kernel[0]) - mixing(spec_imag, inner_kernel[1]) + inner_offset[0]
    )
    pre_imag = (
        mixing(spec_imag, inner_kernel[0]) + mixing(spec_real, inner_kernel[1]) + inner_offset[1]
    )
    hid_real = gelu_value(pre_real).astype(jnp.bfloat16)
    hid_imag = gelu_value(pre_imag).astype(jnp.bfloat16)
    out_real = (
        mixing(hid_real, outer_kernel[0]) - mixing(hid_imag, outer_kernel[1]) + outer_offset[0]
    )
    out_imag = (
        mixing(hid_imag, outer_kernel[0]) + mixing(hid_real, outer_kernel[1]) + outer_offset[1]
    )
    filtered = jnp.stack([shrink(out_real), shrink(out_imag)])
    back_real = (cotangent[0].astype(jnp.float32) * shrink_slope(out_real)).astype(jnp.bfloat16)
    back_imag = (cotangent[1].astype(jnp.float32) * shrink_slope(out_imag)).astype(jnp.bfloat16)
    outer_grad = jnp.stack(
        [
            crossed(hid_real, back_real) + crossed(hid_imag, back_imag),
            crossed(hid_real, back_imag) - crossed(hid_imag, back_real),
        ]
    )
    outer_bias = jnp.stack(
        [
            jnp.sum(back_real, axis=0, dtype=jnp.float32),
            jnp.sum(back_imag, axis=0, dtype=jnp.float32),
        ]
    )
    grad_real = (
        (backmix(back_real, outer_kernel[0]) + backmix(back_imag, outer_kernel[1]))
        * gelu_slope(pre_real)
    ).astype(jnp.bfloat16)
    grad_imag = (
        (backmix(back_imag, outer_kernel[0]) - backmix(back_real, outer_kernel[1]))
        * gelu_slope(pre_imag)
    ).astype(jnp.bfloat16)
    inner_grad = jnp.stack(
        [
            crossed(spec_real, grad_real) + crossed(spec_imag, grad_imag),
            crossed(spec_real, grad_imag) - crossed(spec_imag, grad_real),
        ]
    )
    inner_bias = jnp.stack(
        [
            jnp.sum(grad_real, axis=0, dtype=jnp.float32),
            jnp.sum(grad_imag, axis=0, dtype=jnp.float32),
        ]
    )
    return (filtered, (inner_grad, inner_bias, outer_grad, outer_bias))


def per_device(fields, spec_cotangent, inner_kernel, inner_offset, outer_kernel, outer_offset):
    lat_devices = lax.axis_size("lat")
    lon_devices = lax.axis_size("lon")
    conditions = fields.shape[0]
    height = fields.shape[1] * lat_devices
    width = fields.shape[2] * lon_devices
    wavenumbers = width // 2
    cosine_rows, sine_rows = dft_tables(height, height)
    cosine_cols, sine_cols = dft_tables(width, wavenumbers)
    arriving = lax.all_to_all(fields, "lat", split_axis=3, concat_axis=1, tiled=True)
    shape_in = arriving.shape
    floats = arriving.astype(jnp.float32).reshape(
        shape_in[0], shape_in[1], shape_in[2] * shape_in[3]
    )
    real_part = jnp.einsum("bhx,hm->bmx", floats, cosine_rows, precision=precise)
    imag_part = -jnp.einsum("bhx,hm->bmx", floats, sine_rows, precision=precise)
    spec_rows = jnp.stack([real_part, imag_part]).reshape((2,) + shape_in)
    arriving = lax.all_to_all(spec_rows, "lon", split_axis=2, concat_axis=3, tiled=True)
    real_part = jnp.einsum(
        "bhwd,wk->bhkd", arriving[0], cosine_cols, precision=precise
    ) + jnp.einsum("bhwd,wk->bhkd", arriving[1], sine_cols, precision=precise)
    imag_part = jnp.einsum(
        "bhwd,wk->bhkd", arriving[1], cosine_cols, precision=precise
    ) - jnp.einsum("bhwd,wk->bhkd", arriving[0], sine_cols, precision=precise)
    spec_half = jnp.stack([real_part, imag_part]).astype(jnp.bfloat16)
    spectrum = lax.all_to_all(spec_half, "lat", split_axis=3, concat_axis=4, tiled=True)
    blocks = inner_kernel.shape[1]
    block_width = inner_kernel.shape[2]
    local_shape = spectrum.shape
    flat_spec = spectrum.reshape(2, -1, blocks, block_width)
    flat_cot = spec_cotangent.reshape(2, -1, blocks, block_width)
    filtered, gradients = block_filter(
        flat_spec, flat_cot, inner_kernel, inner_offset, outer_kernel, outer_offset
    )
    totals = lax.psum((gradients[0], gradients[1], gradients[2], gradients[3]), ("lat", "lon"))
    normalizer = 1.0 / math.sqrt(conditions * height * wavenumbers)
    return (
        filtered.reshape(local_shape),
        totals[0] * normalizer,
        totals[1] * normalizer,
        totals[2] * normalizer,
        totals[3] * normalizer,
    )


def split_table(table):
    high = table.astype(jnp.bfloat16)
    low = (table - high.astype(np.float64)).astype(jnp.bfloat16)
    return np.stack([high, low])


def phase_tables(length, columns):
    product = np.arange(length)[:, None] * np.arange(columns)[None, :] % length
    angles = product * (2.0 * math.pi / length)
    return np.cos(angles) / math.sqrt(length), np.sin(angles) / math.sqrt(length)


def column_tables(width, wavenumbers, groups):
    cosine, sine = phase_tables(width, wavenumbers)
    both = np.stack([cosine.T, -sine.T]).reshape(2, groups, wavenumbers // groups, width)
    return split_table(both.transpose(1, 0, 2, 3).reshape(2 * wavenumbers, width))


def row_tables(height, inner):
    cosine, sine = phase_tables(height, height)
    eye = np.eye(inner)
    both = np.stack([cosine.T, sine.T])
    scales = np.linspace(1.0, 2.0, 2001)
    errors = [
        np.mean(((both * a).astype(jnp.bfloat16).astype(np.float64) / a - both) ** 2) for a in scales
    ]
    scale = float(scales[int(np.argmin(errors))])
    return np.stack([np.kron(part * scale, eye) for part in both]).astype(jnp.bfloat16), 1.0 / scale


def padded(values, lanes):
    rows, columns = values.shape
    return jnp.concatenate([values, jnp.zeros((rows, lanes - columns), values.dtype)], axis=1)


def fold(matrix, bias, lanes):
    width = matrix.shape[0]
    side = lanes - width
    keep = width * width // lanes
    rest = matrix[keep:]
    tail = jnp.concatenate(
        [rest[:, t * side : (t + 1) * side] for t in range(width // side)], axis=0
    )
    top = jnp.concatenate([matrix[:keep], tail], axis=1)
    return jnp.concatenate([top, bias], axis=0)


def two_halves(pair, width, lanes):
    rows = pair.shape[0] // 2
    return jnp.concatenate(
        [
            pair[half * rows : (half + 1) * rows, p * lanes : p * lanes + width]
            for half in range(2)
            for p in range(2)
        ],
        axis=1,
    )


def unpack_kernel(
    gather_hbm,
    arrived_hbm,
    filt_hbm,
    inner_hbm,
    inner_off_hbm,
    outer_hbm,
    outer_off_hbm,
    gather_ref,
    arrived_ref,
    filt_ref,
    grad_ref,
    off_ref,
    sems,
):
    blocks = arrived_ref.shape[0]
    width = grad_ref.shape[2]
    lanes = gather_ref.shape[-1]
    side = lanes - width
    keep = width * width // lanes
    step = width - keep
    f32 = jnp.float32
    m_local, k_local = filt_ref.shape[1:3]
    loads = [
        pltpu.make_async_copy(arrived_hbm, arrived_ref, sems.at[0]),
        pltpu.make_async_copy(gather_hbm, gather_ref, sems.at[1]),
    ]
    for load in loads:
        load.start()
    stores = []
    loads[0].wait()
    groups = [arrived_ref[b].astype(f32) for b in range(blocks)]
    for p in range(2):
        for half in range(2):
            first = (2 * half + p) * width
            whole = jnp.concatenate([group[:, first : first + width] for group in groups], axis=1)
            for m in range(m_local // 2):
                filt_ref[p, half * (m_local // 2) + m] = whole[m * k_local : (m + 1) * k_local]
        stores.append(pltpu.make_async_copy(filt_ref.at[p], filt_hbm.at[p], sems.at[2 + p]))
        stores[-1].start()
    loads[1].wait()
    for q in range(4):
        for b in range(blocks):
            piece = gather_ref[b % 2, q, b // 2].astype(f32)
            grad_ref[q, b, 0:keep, :] = piece[0:keep, 0:width]
            grad_ref[q, b, keep:width, :] = jnp.concatenate(
                [piece[t * step : (t + 1) * step, width:lanes] for t in range(width // side)], axis=1
            )
            off_ref[q, b : b + 1, :] = piece[keep : keep + 1, 0:width]
        grad = inner_hbm if q < 2 else outer_hbm
        off = inner_off_hbm if q < 2 else outer_off_hbm
        stores.append(pltpu.make_async_copy(grad_ref.at[q], grad.at[q % 2], sems.at[4 + q]))
        stores.append(pltpu.make_async_copy(off_ref.at[q], off.at[q % 2], sems.at[8 + q]))
        stores[-2].start()
        stores[-1].start()
    for store in stores:
        store.wait()


def fused_kernel(
    sizes,
    fields_hbm,
    cot_hbm,
    inner_ref,
    inner_off_hbm,
    outer_ref,
    outer_off_hbm,
    cols_hbm,
    rows_hbm,
    gather,
    recv_d,
    send_a,
    recv_a,
    send_b,
    recv_b,
    send_c,
    recv_c,
    send_d,
    send_e,
    recv_e,
    spec_s,
    hid_s,
    back_s,
    hb_s,
    raw_w,
    w1,
    w2,
    rows_ref,
    cols_ref,
    fields_ref,
    cot_ref,
    inner_off_ref,
    outer_off_ref,
    lon_send,
    lon_recv,
    lat_send,
    lat_recv,
    z_send,
    z_recv,
    spread_send,
    spread_recv,
    core_send,
    core_recv,
    local_sem,
):
    lats, lons, blocks, width, lanes, normalizer, unscale = sizes
    i = lax.axis_index("lat")
    j = lax.axis_index("lon")
    h_local = fields_ref.shape[0]
    m_local, k_local = cot_ref.shape[1], cot_ref.shape[2]
    tokens = spec_s.shape[0]
    part_rows = m_local * k_local
    zs = lons // 2
    f32, bf16 = jnp.float32, jnp.bfloat16
    mesh_id = pl.DeviceIdType.MESH

    barrier = pltpu.get_barrier_semaphore()

    def greet_lon(d, carry):
        pl.semaphore_signal(
            barrier, inc=1, device_id=(i, lax.rem(j + d, lons)), device_id_type=mesh_id
        )
        return carry

    def greet_lat(d, carry):
        pl.semaphore_signal(
            barrier, inc=1, device_id=(lax.rem(i + d, lats), j), device_id_type=mesh_id
        )
        return carry

    sources = [
        (fields_hbm, fields_ref),
        (cot_hbm, cot_ref),
        (cols_hbm, cols_ref),
        (inner_off_hbm, inner_off_ref),
        (outer_off_hbm, outer_off_ref),
        (inner_ref.at[0, j], raw_w.at[0]),
        (inner_ref.at[1, j], raw_w.at[1]),
        (outer_ref.at[0, j], raw_w.at[2]),
        (outer_ref.at[1, j], raw_w.at[3]),
        (rows_hbm, rows_ref),
    ]
    loads = [
        pltpu.make_async_copy(source, target, local_sem.at[n])
        for n, (source, target) in enumerate(sources)
    ]
    loads[0].start()
    lax.fori_loop(1, lons, greet_lon, 0)
    lax.fori_loop(1, lats, greet_lat, 0)
    for load in loads[1:]:
        load.start()
    loads[0].wait()

    rows_of = [fields_ref[h].astype(f32) for h in range(h_local)]
    for b in range(blocks):
        send_a[b] = jnp.concatenate(
            [row[:, b * width : (b + 1) * width] for row in rows_of], axis=1
        ).astype(bf16)

    pl.semaphore_wait(barrier, lons + lats - 2)

    def lon_copy(phase, src, dst, d):
        return pltpu.make_async_remote_copy(
            src_ref=src,
            dst_ref=dst,
            send_sem=lon_send.at[phase, d],
            recv_sem=lon_recv.at[phase, d],
            device_id=(i, lax.rem(j + d, lons)),
            device_id_type=mesh_id,
        )

    def lat_copy(phase, src, dst, d):
        return pltpu.make_async_remote_copy(
            src_ref=src,
            dst_ref=dst,
            send_sem=lat_send.at[phase, d],
            recv_sem=lat_recv.at[phase, d],
            device_id=(lax.rem(i + d, lats), j),
            device_id_type=mesh_id,
        )

    def exchange_start(copy, phase, send, recv, me, n):
        def one(d, carry):
            copy(phase, send.at[lax.rem(me + d, n)], recv.at[me], d).start()
            return carry

        lax.fori_loop(1, n, one, 0)

    def exchange_recv(copy, phase, send, recv, me, n):
        def one(d, carry):
            source = lax.rem(me + n - d, n)
            copy(phase, send.at[source], recv.at[source], d).wait_recv()
            return carry

        lax.fori_loop(1, n, one, 0)

    def exchange_sent(copy, phase, send, recv, me, n):
        def one(d, carry):
            copy(phase, send.at[lax.rem(me + d, n)], recv.at[me], d).wait_send()
            return carry

        lax.fori_loop(1, n, one, 0)

    exchange_start(lon_copy, 0, send_a, recv_a, j, lons)
    recv_a[j] = send_a[j]

    loads[1].wait()
    quarters = [
        jnp.concatenate(
            [cot_ref[p, half * (m_local // 2) + m].astype(f32) for m in range(m_local // 2)], axis=0
        )
        for half in range(2)
        for p in range(2)
    ]
    for b in range(blocks):
        send_c[b] = jnp.concatenate(
            [part[:, b * width : (b + 1) * width] for part in quarters], axis=1
        ).astype(bf16)
    recv_c[j] = send_c[j]

    for load in loads[2:]:
        load.wait()
    w1[...] = jnp.zeros_like(w1)
    w2[...] = jnp.zeros_like(w2)
    for target, base in ((w1, 0), (w2, 2)):
        real, imag = raw_w[base], raw_w[base + 1]
        target[0:width, 0:width] = real
        target[0:width, lanes : lanes + width] = imag
        target[lanes : lanes + width, 0:width] = -imag
        target[lanes : lanes + width, lanes : lanes + width] = real
    off1 = jnp.concatenate(
        [padded(inner_off_ref[p, pl.ds(j, 1), :], lanes) for p in range(2)], axis=1
    )
    off2 = jnp.concatenate(
        [padded(outer_off_ref[p, pl.ds(j, 1), :], lanes) for p in range(2)], axis=1
    )

    exchange_recv(lon_copy, 0, send_a, recv_a, j, lons)
    exchange_start(lon_copy, 1, send_c, recv_c, j, lons)
    columns = jnp.concatenate([recv_a[s].astype(f32) for s in range(lons)], axis=0).astype(bf16)
    half = jnp.dot(cols_ref[0], columns, preferred_element_type=f32) + jnp.dot(
        cols_ref[1], columns, preferred_element_type=f32
    )
    for g in range(lats):
        high, low = [], []
        for p in range(2):
            first = (2 * g + p) * k_local
            value = jnp.concatenate(
                [
                    half[first : first + k_local, h * width : (h + 1) * width]
                    for h in range(h_local)
                ],
                axis=0,
            )
            top = value.astype(bf16).astype(f32)
            high.append(top)
            low.append(value - top)
        send_b[g] = jnp.concatenate(high + low, axis=1).astype(bf16)

        @pl.when(g != i)
        def _():
            lat_copy(0, send_b.at[g], recv_b.at[i], lax.rem(g - i + lats, lats)).start()

    recv_b[i] = send_b[i]
    exchange_recv(lat_copy, 0, send_b, recv_b, i, lats)

    chunks = 4
    chunk = tokens // chunks
    per_chunk = lons // chunks
    packed = jnp.concatenate([recv_b[s].astype(f32) for s in range(lats)], axis=0)
    lines = jnp.concatenate(
        [padded(packed[:, t * width : (t + 1) * width], lanes) for t in range(4)], axis=1
    ).astype(bf16)
    ones_lane = lax.broadcasted_iota(jnp.int32, (chunk, 2 * lanes), 1) == width
    one = jnp.ones((chunk, 2 * lanes), f32)
    for c in range(chunks):
        rows = slice(c * chunk, (c + 1) * chunk)
        cos_part = jnp.dot(rows_ref[0, rows, :], lines, preferred_element_type=f32)
        sin_part = jnp.dot(rows_ref[1, rows, :], lines, preferred_element_type=f32)
        cos_part = cos_part[:, : 2 * lanes] + cos_part[:, 2 * lanes :]
        sin_part = sin_part[:, : 2 * lanes] + sin_part[:, 2 * lanes :]
        real = cos_part[:, :lanes] + sin_part[:, lanes:]
        imag = cos_part[:, lanes:] - sin_part[:, :lanes]
        spec_wide = jnp.concatenate([real, imag], axis=1) * unscale
        spec = spec_wide.astype(bf16)
        spec_s[rows, :] = jnp.where(ones_lane, one, spec_wide).astype(bf16)
        pre = jnp.dot(spec, w1[...], preferred_element_type=f32) + off1
        square = pre * pre
        level = jnp.tanh(gelu_coeff * (pre + 0.044715 * pre * square))
        hid_wide = 0.5 * pre * (1.0 + level)
        slope = 0.5 * (1.0 + level) + 0.5 * pre * (1.0 - level * level) * gelu_coeff * (
            1.0 + 3.0 * 0.044715 * square
        )
        hid_s[rows, :] = jnp.where(ones_lane, one, hid_wide).astype(bf16)
        out = jnp.dot(hid_wide.astype(bf16), w2[...], preferred_element_type=f32) + off2
        soft = jnp.tanh(out * (1.0 / shrink_level))
        filtered = out - shrink_level * soft
        for r in range(per_chunk):
            dest = c * per_chunk + r
            send_d[dest] = two_halves(
                filtered[r * part_rows : (r + 1) * part_rows], width, lanes
            ).astype(bf16)

            @pl.when(dest != j)
            def _():
                away = lax.rem(dest - j + lons, lons)
                lon_copy(2, send_d.at[dest], recv_d.at[j], away).start()

        if c == 0:
            exchange_recv(lon_copy, 1, send_c, recv_c, j, lons)
        parts = []
        for r in range(per_chunk):
            group = recv_c[c * per_chunk + r].astype(f32)
            fours = [padded(group[:, t * width : (t + 1) * width], lanes) for t in range(4)]
            parts.append(jnp.concatenate(fours[0:2], axis=1))
            parts.append(jnp.concatenate(fours[2:4], axis=1))
        cot = jnp.concatenate(parts, axis=0)
        back = (cot * (soft * soft)).astype(bf16)
        back_s[rows, :] = back
        turned = lax.dot_general(
            back, w2[...], (((1,), (1,)), ((), ())), preferred_element_type=f32
        )
        hb_s[rows, :] = (turned * slope).astype(bf16)
    recv_d[j] = send_d[j]

    extra = send_e.shape[1] - width * width // lanes
    for base, left, right in ((2, hid_s, back_s), (0, spec_s, hb_s)):
        full = lax.dot_general(
            left[...], right[...], (((0,), (0,)), ((), ())), preferred_element_type=f32
        )
        first = full[:lanes, :lanes] + full[lanes:, lanes:]
        second = full[:lanes, lanes:] - full[lanes:, :lanes]
        for n, value in enumerate((first, second)):
            send_e[base + n] = fold(
                value[:width, :width], value[width : width + extra], lanes
            ).astype(bf16)
    exchange_start(lat_copy, 1, send_e, recv_e, i, lats)
    recv_e[i] = send_e[i]
    exchange_recv(lat_copy, 1, send_e, recv_e, i, lats)
    total = recv_e[0].astype(f32)
    for s in range(1, lats):
        total = total + recv_e[s].astype(f32)
    side = lax.rem(j, 2)
    z = lax.div(j, 2)
    gather[side, i, z] = (total * normalizer).astype(bf16)

    def z_copy(d, slot):
        return pltpu.make_async_remote_copy(
            src_ref=gather.at[side, i, slot],
            dst_ref=gather.at[side, i, slot],
            send_sem=z_send.at[d],
            recv_sem=z_recv.at[d],
            device_id=(i, lax.rem(j + 2 * d, lons)),
            device_id_type=mesh_id,
        )

    def spread_copy(d, row, slot, turn):
        return pltpu.make_async_remote_copy(
            src_ref=gather.at[side, row, slot],
            dst_ref=gather.at[side, row, slot],
            send_sem=spread_send.at[turn, d],
            recv_sem=spread_recv.at[turn, d],
            device_id=(lax.rem(i + d, lats), j),
            device_id_type=mesh_id,
        )

    def side_copy(from_side, slot):
        return pltpu.make_async_remote_copy(
            src_ref=gather.at[from_side, slot],
            dst_ref=gather.at[from_side, slot],
            send_sem=core_send.at[slot],
            recv_sem=core_recv.at[slot],
            device_id=(i, j + 1 - 2 * side),
            device_id_type=mesh_id,
        )

    for d in range(1, zs):
        z_copy(d, z).start()
    for turn in range(zs):
        slot = lax.rem(z + zs - turn, zs)
        if turn:
            z_copy(turn, slot).wait_recv()
        for d in range(1, lats):
            spread_copy(d, i, slot, turn).start()
    side_copy(side, i).start()
    for d in range(1, lats):
        source = lax.rem(i + lats - d, lats)
        for turn in range(zs):
            spread_copy(d, source, lax.rem(z + zs - turn, zs), turn).wait_recv()
        side_copy(side, source).start()

    exchange_recv(lon_copy, 2, send_d, recv_d, j, lons)
    exchange_sent(lon_copy, 0, send_a, recv_a, j, lons)
    exchange_sent(lon_copy, 1, send_c, recv_c, j, lons)
    exchange_sent(lon_copy, 2, send_d, recv_d, j, lons)
    exchange_sent(lat_copy, 0, send_b, recv_b, i, lats)
    exchange_sent(lat_copy, 1, send_e, recv_e, i, lats)
    for d in range(1, zs):
        z_copy(d, z).wait_send()
    for turn in range(zs):
        for d in range(1, lats):
            spread_copy(d, i, lax.rem(z + zs - turn, zs), turn).wait_send()
    for q in range(lats):
        side_copy(side, q).wait_send()
    for q in range(lats):
        side_copy(1 - side, q).wait_recv()


def fused_device(fields, spec_cotangent, inner_kernel, inner_offset, outer_kernel, outer_offset):
    lats = lax.axis_size("lat")
    lons = lax.axis_size("lon")
    _, h_local, w_local, channels = fields.shape
    m_local, k_local = spec_cotangent.shape[2:4]
    blocks, width = inner_kernel.shape[1:3]
    height, full_width = h_local * lats, w_local * lons
    wavenumbers = k_local * lats
    lanes = 128
    tokens = height * k_local
    part_rows = m_local * k_local
    deep = width * width // lanes + 8
    normalizer = 1.0 / math.sqrt(height * wavenumbers)
    cols = jnp.asarray(column_tables(full_width, wavenumbers, lats))
    rows, unscale = row_tables(height, k_local)
    rows = jnp.asarray(rows)
    vmem = pl.BlockSpec(memory_space=pltpu.VMEM)
    hbm = pl.BlockSpec(memory_space=pltpu.HBM)
    bf16, f32 = jnp.bfloat16, jnp.float32
    wide = (tokens, 2 * lanes)
    dma = pltpu.SemaphoreType.DMA

    def pair(*shape):
        return [pltpu.VMEM(shape, bf16)] * 2

    gathered, arrived = pl.pallas_call(
        lambda *refs: fused_kernel(
            (lats, lons, blocks, width, lanes, normalizer, unscale), *refs
        ),
        name="fused_filter",
        out_shape=[
            jax.ShapeDtypeStruct((2, lats, lons // 2, deep, lanes), bf16),
            jax.ShapeDtypeStruct((blocks, part_rows // 2, 4 * width), bf16),
        ],
        in_specs=[hbm] * 8,
        out_specs=[vmem] * 2,
        scratch_shapes=[
            *pair(blocks, w_local, h_local * width),
            *pair(lats, h_local * k_local, 4 * width),
            *pair(blocks, part_rows // 2, 4 * width),
            pltpu.VMEM((blocks, part_rows // 2, 4 * width), bf16),
            *pair(4, deep, lanes),
            *[pltpu.VMEM(wide, bf16)] * 4,
            pltpu.VMEM((4, width, width), bf16),
            *pair(2 * lanes, 2 * lanes),
            pltpu.VMEM(rows.shape, bf16),
            pltpu.VMEM(cols.shape, bf16),
            pltpu.VMEM(fields.shape[1:], bf16),
            pltpu.VMEM((2, m_local, k_local, channels), bf16),
            pltpu.VMEM(inner_offset.shape, f32),
            pltpu.VMEM(outer_offset.shape, f32),
            dma((3, lons)),
            dma((3, lons)),
            dma((2, lats)),
            dma((2, lats)),
            dma((lons // 2,)),
            dma((lons // 2,)),
            dma((lons // 2, lats)),
            dma((lons // 2, lats)),
            dma((lats,)),
            dma((lats,)),
            dma((10,)),
        ],
        compiler_params=pltpu.CompilerParams(
            collective_id=0, has_side_effects=True, vmem_limit_bytes=63 * 1024 * 1024
        ),
    )(
        fields.reshape(fields.shape[1:]),
        spec_cotangent.reshape(2, m_local, k_local, channels),
        inner_kernel,
        inner_offset,
        outer_kernel,
        outer_offset,
        cols,
        rows,
    )
    filt, inner_grad, inner_bias, outer_grad, outer_bias = pl.pallas_call(
        unpack_kernel,
        name="unpack",
        out_shape=[
            jax.ShapeDtypeStruct((2, m_local, k_local, channels), f32),
            jax.ShapeDtypeStruct(inner_kernel.shape, f32),
            jax.ShapeDtypeStruct(inner_offset.shape, f32),
            jax.ShapeDtypeStruct(outer_kernel.shape, f32),
            jax.ShapeDtypeStruct(outer_offset.shape, f32),
        ],
        in_specs=[hbm] * 2,
        out_specs=[hbm] * 5,
        scratch_shapes=[
            pltpu.VMEM(gathered.shape, bf16),
            pltpu.VMEM(arrived.shape, bf16),
            pltpu.VMEM((2, m_local, k_local, channels), f32),
            pltpu.VMEM((4, blocks, width, width), f32),
            pltpu.VMEM((4, blocks, width), f32),
            dma((12,)),
        ],
        compiler_params=pltpu.CompilerParams(vmem_limit_bytes=63 * 1024 * 1024),
    )(gathered, arrived)
    return (
        filt.reshape(spec_cotangent.shape),
        inner_grad,
        inner_bias,
        outer_grad,
        outer_bias,
    )


def choose_device(fields, spec_cotangent, inner_kernel, *rest):
    lats, lons = lax.axis_size("lat"), lax.axis_size("lon")
    blocks, width = inner_kernel.shape[1:3]
    fits = (
        fields.shape[0] == 1
        and lons == blocks
        and lats == 4
        and width == 96
        and fields.shape[1] == 16
        and fields.shape[2] == 8
        and spec_cotangent.shape[2] == 8
        and spec_cotangent.shape[3] == 8
    )
    chosen = fused_device if fits else per_device
    return chosen(fields, spec_cotangent, inner_kernel, *rest)


def solution(mesh):
    placed = (P(None, "lat", "lon", None), P(None, None, "lon", "lat", None), P(), P(), P(), P())
    return jax.shard_map(
        choose_device,
        mesh=mesh,
        in_specs=placed,
        out_specs=(P(None, None, "lon", "lat", None), P(), P(), P(), P()),
        check_vma=False,
    )
```

```python
import math

import jax
import jax.numpy as jnp
import numpy as np
from jax import lax
from jax.experimental import pallas as pl
from jax.experimental.pallas import tpu as pltpu
from jax.sharding import PartitionSpec as P

shrink_level = 0.1
gelu_coeff = 0.7978845608028654
precise = lax.Precision.HIGHEST


def dft_tables(length, columns):
    points = jnp.arange(length, dtype=jnp.int32)
    orders = jnp.arange(columns, dtype=jnp.int32)
    product = points[:, None] * orders[None, :] % length
    angles = product.astype(jnp.float32) * (2.0 * math.pi / length)
    factor = 1.0 / math.sqrt(length)
    return (jnp.cos(angles) * factor, jnp.sin(angles) * factor)


def shrink(values):
    return values - shrink_level * jnp.tanh(values / shrink_level)


def shrink_slope(values):
    level = jnp.tanh(values / shrink_level)
    return level * level


def gelu_value(values):
    inner = gelu_coeff * (values + 0.044715 * values * values * values)
    return 0.5 * values * (1.0 + jnp.tanh(inner))


def gelu_slope(values):
    inner = gelu_coeff * (values + 0.044715 * values * values * values)
    level = jnp.tanh(inner)
    return 0.5 * (1.0 + level) + 0.5 * values * (1.0 - level * level) * gelu_coeff * (
        1.0 + 3.0 * 0.044715 * values * values
    )


def mixing(operand, kernel):
    return jnp.einsum("rnb,nbc->rnc", operand, kernel, preferred_element_type=jnp.float32)


def backmix(operand, kernel):
    return jnp.einsum("rnc,nbc->rnb", operand, kernel, preferred_element_type=jnp.float32)


def crossed(operand, second):
    return jnp.einsum("rnb,rnc->nbc", operand, second, preferred_element_type=jnp.float32)


def block_filter(spectrum, cotangent, inner_kernel, inner_offset, outer_kernel, outer_offset):
    spec_real, spec_imag = (spectrum[0], spectrum[1])
    pre_real = (
        mixing(spec_real, inner_kernel[0]) - mixing(spec_imag, inner_kernel[1]) + inner_offset[0]
    )
    pre_imag = (
        mixing(spec_imag, inner_kernel[0]) + mixing(spec_real, inner_kernel[1]) + inner_offset[1]
    )
    hid_real = gelu_value(pre_real).astype(jnp.bfloat16)
    hid_imag = gelu_value(pre_imag).astype(jnp.bfloat16)
    out_real = (
        mixing(hid_real, outer_kernel[0]) - mixing(hid_imag, outer_kernel[1]) + outer_offset[0]
    )
    out_imag = (
        mixing(hid_imag, outer_kernel[0]) + mixing(hid_real, outer_kernel[1]) + outer_offset[1]
    )
    filtered = jnp.stack([shrink(out_real), shrink(out_imag)])
    back_real = (cotangent[0].astype(jnp.float32) * shrink_slope(out_real)).astype(jnp.bfloat16)
    back_imag = (cotangent[1].astype(jnp.float32) * shrink_slope(out_imag)).astype(jnp.bfloat16)
    outer_grad = jnp.stack(
        [
            crossed(hid_real, back_real) + crossed(hid_imag, back_imag),
            crossed(hid_real, back_imag) - crossed(hid_imag, back_real),
        ]
    )
    outer_bias = jnp.stack(
        [
            jnp.sum(back_real, axis=0, dtype=jnp.float32),
            jnp.sum(back_imag, axis=0, dtype=jnp.float32),
        ]
    )
    grad_real = (
        (backmix(back_real, outer_kernel[0]) + backmix(back_imag, outer_kernel[1]))
        * gelu_slope(pre_real)
    ).astype(jnp.bfloat16)
    grad_imag = (
        (backmix(back_imag, outer_kernel[0]) - backmix(back_real, outer_kernel[1]))
        * gelu_slope(pre_imag)
    ).astype(jnp.bfloat16)
    inner_grad = jnp.stack(
        [
            crossed(spec_real, grad_real) + crossed(spec_imag, grad_imag),
            crossed(spec_real, grad_imag) - crossed(spec_imag, grad_real),
        ]
    )
    inner_bias = jnp.stack(
        [
            jnp.sum(grad_real, axis=0, dtype=jnp.float32),
            jnp.sum(grad_imag, axis=0, dtype=jnp.float32),
        ]
    )
    return (filtered, (inner_grad, inner_bias, outer_grad, outer_bias))


def per_device(fields, spec_cotangent, inner_kernel, inner_offset, outer_kernel, outer_offset):
    lat_devices = lax.axis_size("lat")
    lon_devices = lax.axis_size("lon")
    conditions = fields.shape[0]
    height = fields.shape[1] * lat_devices
    width = fields.shape[2] * lon_devices
    wavenumbers = width // 2
    cosine_rows, sine_rows = dft_tables(height, height)
    cosine_cols, sine_cols = dft_tables(width, wavenumbers)
    arriving = lax.all_to_all(fields, "lat", split_axis=3, concat_axis=1, tiled=True)
    shape_in = arriving.shape
    floats = arriving.astype(jnp.float32).reshape(
        shape_in[0], shape_in[1], shape_in[2] * shape_in[3]
    )
    real_part = jnp.einsum("bhx,hm->bmx", floats, cosine_rows, precision=precise)
    imag_part = -jnp.einsum("bhx,hm->bmx", floats, sine_rows, precision=precise)
    spec_rows = jnp.stack([real_part, imag_part]).reshape((2,) + shape_in)
    arriving = lax.all_to_all(spec_rows, "lon", split_axis=2, concat_axis=3, tiled=True)
    real_part = jnp.einsum(
        "bhwd,wk->bhkd", arriving[0], cosine_cols, precision=precise
    ) + jnp.einsum("bhwd,wk->bhkd", arriving[1], sine_cols, precision=precise)
    imag_part = jnp.einsum(
        "bhwd,wk->bhkd", arriving[1], cosine_cols, precision=precise
    ) - jnp.einsum("bhwd,wk->bhkd", arriving[0], sine_cols, precision=precise)
    spec_half = jnp.stack([real_part, imag_part]).astype(jnp.bfloat16)
    spectrum = lax.all_to_all(spec_half, "lat", split_axis=3, concat_axis=4, tiled=True)
    blocks = inner_kernel.shape[1]
    block_width = inner_kernel.shape[2]
    local_shape = spectrum.shape
    flat_spec = spectrum.reshape(2, -1, blocks, block_width)
    flat_cot = spec_cotangent.reshape(2, -1, blocks, block_width)
    filtered, gradients = block_filter(
        flat_spec, flat_cot, inner_kernel, inner_offset, outer_kernel, outer_offset
    )
    totals = lax.psum((gradients[0], gradients[1], gradients[2], gradients[3]), ("lat", "lon"))
    normalizer = 1.0 / math.sqrt(conditions * height * wavenumbers)
    return (
        filtered.reshape(local_shape),
        totals[0] * normalizer,
        totals[1] * normalizer,
        totals[2] * normalizer,
        totals[3] * normalizer,
    )


def split_table(table):
    high = table.astype(jnp.bfloat16)
    low = (table - high.astype(np.float64)).astype(jnp.bfloat16)
    return np.stack([high, low])


def phase_tables(length, columns):
    product = np.arange(length)[:, None] * np.arange(columns)[None, :] % length
    angles = product * (2.0 * math.pi / length)
    return np.cos(angles) / math.sqrt(length), np.sin(angles) / math.sqrt(length)


def column_tables(width, wavenumbers, groups):
    cosine, sine = phase_tables(width, wavenumbers)
    both = np.stack([cosine.T, -sine.T]).reshape(2, groups, wavenumbers // groups, width)
    return split_table(both.transpose(1, 0, 2, 3).reshape(2 * wavenumbers, width))


def row_tables(height, inner):
    cosine, sine = phase_tables(height, height)
    eye = np.eye(inner)
    both = np.stack([cosine.T, sine.T])
    scales = np.linspace(1.0, 2.0, 2001)
    errors = [
        np.mean(((both * a).astype(jnp.bfloat16).astype(np.float64) / a - both) ** 2) for a in scales
    ]
    scale = float(scales[int(np.argmin(errors))])
    return np.stack([np.kron(part * scale, eye) for part in both]).astype(jnp.bfloat16), 1.0 / scale


def padded(values, lanes):
    rows, columns = values.shape
    return jnp.concatenate([values, jnp.zeros((rows, lanes - columns), values.dtype)], axis=1)


def fold(matrix, bias, lanes):
    width = matrix.shape[0]
    side = lanes - width
    keep = width * width // lanes
    rest = matrix[keep:]
    tail = jnp.concatenate(
        [rest[:, t * side : (t + 1) * side] for t in range(width // side)], axis=0
    )
    top = jnp.concatenate([matrix[:keep], tail], axis=1)
    return jnp.concatenate([top, bias], axis=0)


def two_halves(pair, width, lanes):
    rows = pair.shape[0] // 2
    return jnp.concatenate(
        [
            pair[half * rows : (half + 1) * rows, p * lanes : p * lanes + width]
            for half in range(2)
            for p in range(2)
        ],
        axis=1,
    )


def unpack_kernel(
    gather_hbm,
    arrived_hbm,
    filt_hbm,
    inner_hbm,
    inner_off_hbm,
    outer_hbm,
    outer_off_hbm,
    gather_ref,
    arrived_ref,
    filt_ref,
    grad_ref,
    off_ref,
    sems,
):
    blocks = arrived_ref.shape[0]
    width = grad_ref.shape[2]
    lanes = gather_ref.shape[-1]
    side = lanes - width
    keep = width * width // lanes
    step = width - keep
    f32 = jnp.float32
    m_local, k_local = filt_ref.shape[1:3]
    loads = [
        pltpu.make_async_copy(arrived_hbm, arrived_ref, sems.at[0]),
    ] + [
        pltpu.make_async_copy(gather_hbm.at[e, q], gather_ref.at[e, q], sems.at[12 + 2 * q + e])
        for q in range(4)
        for e in range(2)
    ]
    for load in loads:
        load.start()
    stores = []
    loads[0].wait()
    groups = [arrived_ref[b].astype(f32) for b in range(blocks)]
    for p in range(2):
        for half in range(2):
            first = (2 * half + p) * width
            whole = jnp.concatenate([group[:, first : first + width] for group in groups], axis=1)
            for m in range(m_local // 2):
                filt_ref[p, half * (m_local // 2) + m] = whole[m * k_local : (m + 1) * k_local]
        stores.append(pltpu.make_async_copy(filt_ref.at[p], filt_hbm.at[p], sems.at[2 + p]))
        stores[-1].start()
    for q in range(4):
        loads[1 + 2 * q].wait()
        loads[2 + 2 * q].wait()
        for b in range(blocks):
            piece = gather_ref[b % 2, q, b // 2].astype(f32)
            grad_ref[q, b, 0:keep, :] = piece[0:keep, 0:width]
            grad_ref[q, b, keep:width, :] = jnp.concatenate(
                [piece[t * step : (t + 1) * step, width:lanes] for t in range(width // side)], axis=1
            )
            off_ref[q, b : b + 1, :] = piece[keep : keep + 1, 0:width]
        grad = inner_hbm if q < 2 else outer_hbm
        off = inner_off_hbm if q < 2 else outer_off_hbm
        stores.append(pltpu.make_async_copy(grad_ref.at[q], grad.at[q % 2], sems.at[4 + q]))
        stores.append(pltpu.make_async_copy(off_ref.at[q], off.at[q % 2], sems.at[8 + q]))
        stores[-2].start()
        stores[-1].start()
    for store in stores:
        store.wait()


def fused_kernel(
    sizes,
    fields_hbm,
    cot_hbm,
    inner_ref,
    inner_off_hbm,
    outer_ref,
    outer_off_hbm,
    cols_hbm,
    rows_hbm,
    gather_out,
    arrived_out,
    gather,
    recv_d,
    send_a,
    recv_a,
    send_b,
    recv_b,
    send_c,
    recv_c,
    send_d,
    send_e,
    recv_e,
    spec_s,
    hid_s,
    back_s,
    hb_s,
    raw_w,
    w1,
    w2,
    rows_ref,
    cols_ref,
    fields_ref,
    cot_ref,
    inner_off_ref,
    outer_off_ref,
    lon_send,
    lon_recv,
    lat_send,
    lat_recv,
    z_send,
    z_recv,
    spread_send,
    spread_recv,
    core_send,
    core_recv,
    local_sem,
):
    lats, lons, blocks, width, lanes, normalizer, unscale = sizes
    i = lax.axis_index("lat")
    j = lax.axis_index("lon")
    h_local = fields_ref.shape[0]
    m_local, k_local = cot_ref.shape[1], cot_ref.shape[2]
    tokens = spec_s.shape[0]
    part_rows = m_local * k_local
    zs = lons // 2
    f32, bf16 = jnp.float32, jnp.bfloat16
    mesh_id = pl.DeviceIdType.MESH

    barrier = pltpu.get_barrier_semaphore()

    def greet_lon(d, carry):
        pl.semaphore_signal(
            barrier, inc=1, device_id=(i, lax.rem(j + d, lons)), device_id_type=mesh_id
        )
        return carry

    def greet_lat(d, carry):
        pl.semaphore_signal(
            barrier, inc=1, device_id=(lax.rem(i + d, lats), j), device_id_type=mesh_id
        )
        return carry

    sources = [
        (fields_hbm, fields_ref),
        (cot_hbm, cot_ref),
        (cols_hbm, cols_ref),
        (inner_off_hbm, inner_off_ref),
        (outer_off_hbm, outer_off_ref),
        (inner_ref.at[0, j], raw_w.at[0]),
        (inner_ref.at[1, j], raw_w.at[1]),
        (outer_ref.at[0, j], raw_w.at[2]),
        (outer_ref.at[1, j], raw_w.at[3]),
        (rows_hbm, rows_ref),
    ]
    loads = [
        pltpu.make_async_copy(source, target, local_sem.at[n])
        for n, (source, target) in enumerate(sources)
    ]
    loads[0].start()
    lax.fori_loop(1, lons, greet_lon, 0)
    lax.fori_loop(1, lats, greet_lat, 0)
    for load in loads[1:]:
        load.start()
    loads[0].wait()

    rows_of = [fields_ref[h].astype(f32) for h in range(h_local)]
    for b in range(blocks):
        send_a[b] = jnp.concatenate(
            [row[:, b * width : (b + 1) * width] for row in rows_of], axis=1
        ).astype(bf16)

    pl.semaphore_wait(barrier, lons + lats - 2)

    def lon_copy(phase, src, dst, d):
        return pltpu.make_async_remote_copy(
            src_ref=src,
            dst_ref=dst,
            send_sem=lon_send.at[phase, d],
            recv_sem=lon_recv.at[phase, d],
            device_id=(i, lax.rem(j + d, lons)),
            device_id_type=mesh_id,
        )

    def lat_copy(phase, src, dst, d):
        return pltpu.make_async_remote_copy(
            src_ref=src,
            dst_ref=dst,
            send_sem=lat_send.at[phase, d],
            recv_sem=lat_recv.at[phase, d],
            device_id=(lax.rem(i + d, lats), j),
            device_id_type=mesh_id,
        )

    def exchange_start(copy, phase, send, recv, me, n):
        def one(d, carry):
            copy(phase, send.at[lax.rem(me + d, n)], recv.at[me], d).start()
            return carry

        lax.fori_loop(1, n, one, 0)

    def exchange_recv(copy, phase, send, recv, me, n):
        def one(d, carry):
            source = lax.rem(me + n - d, n)
            copy(phase, send.at[source], recv.at[source], d).wait_recv()
            return carry

        lax.fori_loop(1, n, one, 0)

    def exchange_sent(copy, phase, send, recv, me, n):
        def one(d, carry):
            copy(phase, send.at[lax.rem(me + d, n)], recv.at[me], d).wait_send()
            return carry

        lax.fori_loop(1, n, one, 0)

    exchange_start(lon_copy, 0, send_a, recv_a, j, lons)
    recv_a[j] = send_a[j]

    loads[1].wait()
    quarters = [
        jnp.concatenate(
            [cot_ref[p, half * (m_local // 2) + m].astype(f32) for m in range(m_local // 2)], axis=0
        )
        for half in range(2)
        for p in range(2)
    ]
    for b in range(blocks):
        send_c[b] = jnp.concatenate(
            [part[:, b * width : (b + 1) * width] for part in quarters], axis=1
        ).astype(bf16)
    recv_c[j] = send_c[j]

    for load in loads[2:]:
        load.wait()
    w1[...] = jnp.zeros_like(w1)
    w2[...] = jnp.zeros_like(w2)
    for target, base in ((w1, 0), (w2, 2)):
        real, imag = raw_w[base], raw_w[base + 1]
        target[0:width, 0:width] = real
        target[0:width, lanes : lanes + width] = imag
        target[lanes : lanes + width, 0:width] = -imag
        target[lanes : lanes + width, lanes : lanes + width] = real
    off1 = jnp.concatenate(
        [padded(inner_off_ref[p, pl.ds(j, 1), :], lanes) for p in range(2)], axis=1
    )
    off2 = jnp.concatenate(
        [padded(outer_off_ref[p, pl.ds(j, 1), :], lanes) for p in range(2)], axis=1
    )

    exchange_recv(lon_copy, 0, send_a, recv_a, j, lons)
    exchange_start(lon_copy, 1, send_c, recv_c, j, lons)
    columns = jnp.concatenate([recv_a[s].astype(f32) for s in range(lons)], axis=0).astype(bf16)
    half = jnp.dot(cols_ref[0], columns, preferred_element_type=f32) + jnp.dot(
        cols_ref[1], columns, preferred_element_type=f32
    )
    for g in range(lats):
        high, low = [], []
        for p in range(2):
            first = (2 * g + p) * k_local
            value = jnp.concatenate(
                [
                    half[first : first + k_local, h * width : (h + 1) * width]
                    for h in range(h_local)
                ],
                axis=0,
            )
            top = value.astype(bf16).astype(f32)
            high.append(top)
            low.append(value - top)
        send_b[g] = jnp.concatenate(high + low, axis=1).astype(bf16)

        @pl.when(g != i)
        def _():
            lat_copy(0, send_b.at[g], recv_b.at[i], lax.rem(g - i + lats, lats)).start()

    recv_b[i] = send_b[i]
    exchange_recv(lat_copy, 0, send_b, recv_b, i, lats)

    chunks = 4
    chunk = tokens // chunks
    per_chunk = lons // chunks
    packed = jnp.concatenate([recv_b[s].astype(f32) for s in range(lats)], axis=0)
    lines = jnp.concatenate(
        [padded(packed[:, t * width : (t + 1) * width], lanes) for t in range(4)], axis=1
    ).astype(bf16)
    ones_lane = lax.broadcasted_iota(jnp.int32, (chunk, 2 * lanes), 1) == width
    one = jnp.ones((chunk, 2 * lanes), f32)
    for c in range(chunks):
        rows = slice(c * chunk, (c + 1) * chunk)
        cos_part = jnp.dot(rows_ref[0, rows, :], lines, preferred_element_type=f32)
        sin_part = jnp.dot(rows_ref[1, rows, :], lines, preferred_element_type=f32)
        cos_part = cos_part[:, : 2 * lanes] + cos_part[:, 2 * lanes :]
        sin_part = sin_part[:, : 2 * lanes] + sin_part[:, 2 * lanes :]
        real = cos_part[:, :lanes] + sin_part[:, lanes:]
        imag = cos_part[:, lanes:] - sin_part[:, :lanes]
        spec_wide = jnp.concatenate([real, imag], axis=1) * unscale
        spec = spec_wide.astype(bf16)
        spec_s[rows, :] = jnp.where(ones_lane, one, spec_wide).astype(bf16)
        pre = jnp.dot(spec, w1[...], preferred_element_type=f32) + off1
        square = pre * pre
        level = jnp.tanh(gelu_coeff * (pre + 0.044715 * pre * square))
        hid_wide = 0.5 * pre * (1.0 + level)
        slope = 0.5 * (1.0 + level) + 0.5 * pre * (1.0 - level * level) * gelu_coeff * (
            1.0 + 3.0 * 0.044715 * square
        )
        hid_s[rows, :] = jnp.where(ones_lane, one, hid_wide).astype(bf16)
        out = jnp.dot(hid_wide.astype(bf16), w2[...], preferred_element_type=f32) + off2
        soft = jnp.tanh(out * (1.0 / shrink_level))
        filtered = out - shrink_level * soft
        for r in range(per_chunk):
            dest = c * per_chunk + r
            send_d[dest] = two_halves(
                filtered[r * part_rows : (r + 1) * part_rows], width, lanes
            ).astype(bf16)

            @pl.when(dest != j)
            def _():
                away = lax.rem(dest - j + lons, lons)
                lon_copy(2, send_d.at[dest], recv_d.at[j], away).start()

        if c == 0:
            exchange_recv(lon_copy, 1, send_c, recv_c, j, lons)
        parts = []
        for r in range(per_chunk):
            group = recv_c[c * per_chunk + r].astype(f32)
            fours = [padded(group[:, t * width : (t + 1) * width], lanes) for t in range(4)]
            parts.append(jnp.concatenate(fours[0:2], axis=1))
            parts.append(jnp.concatenate(fours[2:4], axis=1))
        cot = jnp.concatenate(parts, axis=0)
        back = (cot * (soft * soft)).astype(bf16)
        back_s[rows, :] = back
        turned = lax.dot_general(
            back, w2[...], (((1,), (1,)), ((), ())), preferred_element_type=f32
        )
        hb_s[rows, :] = (turned * slope).astype(bf16)
    recv_d[j] = send_d[j]

    extra = send_e.shape[1] - width * width // lanes
    for base, left, right in ((2, hid_s, back_s), (0, spec_s, hb_s)):
        full = lax.dot_general(
            left[...], right[...], (((0,), (0,)), ((), ())), preferred_element_type=f32
        )
        first = full[:lanes, :lanes] + full[lanes:, lanes:]
        second = full[:lanes, lanes:] - full[lanes:, :lanes]
        for n, value in enumerate((first, second)):
            send_e[base + n] = fold(
                value[:width, :width], value[width : width + extra], lanes
            ).astype(bf16)
    exchange_start(lat_copy, 1, send_e, recv_e, i, lats)
    recv_e[i] = send_e[i]
    exchange_recv(lat_copy, 1, send_e, recv_e, i, lats)
    total = recv_e[0].astype(f32)
    for s in range(1, lats):
        total = total + recv_e[s].astype(f32)
    side = lax.rem(j, 2)
    z = lax.div(j, 2)
    gather[side, i, z] = (total * normalizer).astype(bf16)

    def z_copy(d, slot):
        return pltpu.make_async_remote_copy(
            src_ref=gather.at[side, i, slot],
            dst_ref=gather.at[side, i, slot],
            send_sem=z_send.at[d],
            recv_sem=z_recv.at[d],
            device_id=(i, lax.rem(j + 2 * d, lons)),
            device_id_type=mesh_id,
        )

    def spread_copy(d, row, slot, turn):
        return pltpu.make_async_remote_copy(
            src_ref=gather.at[side, row, slot],
            dst_ref=gather.at[side, row, slot],
            send_sem=spread_send.at[turn, d],
            recv_sem=spread_recv.at[turn, d],
            device_id=(lax.rem(i + d, lats), j),
            device_id_type=mesh_id,
        )

    def side_copy(from_side, slot):
        return pltpu.make_async_remote_copy(
            src_ref=gather.at[from_side, slot],
            dst_ref=gather.at[from_side, slot],
            send_sem=core_send.at[slot],
            recv_sem=core_recv.at[slot],
            device_id=(i, j + 1 - 2 * side),
            device_id_type=mesh_id,
        )

    for d in range(1, zs):
        z_copy(d, z).start()
    for turn in range(zs):
        slot = lax.rem(z + zs - turn, zs)
        if turn:
            z_copy(turn, slot).wait_recv()
        for d in range(1, lats):
            spread_copy(d, i, slot, turn).start()
    side_copy(side, i).start()
    for d in range(1, lats):
        source = lax.rem(i + lats - d, lats)
        for turn in range(zs):
            spread_copy(d, source, lax.rem(z + zs - turn, zs), turn).wait_recv()
        side_copy(side, source).start()

    exchange_recv(lon_copy, 2, send_d, recv_d, j, lons)
    leaving = [pltpu.make_async_copy(recv_d, arrived_out, local_sem.at[10])]
    leaving.append(pltpu.make_async_copy(gather.at[side], gather_out.at[side], local_sem.at[11]))
    for store in leaving:
        store.start()
    exchange_sent(lon_copy, 0, send_a, recv_a, j, lons)
    exchange_sent(lon_copy, 1, send_c, recv_c, j, lons)
    exchange_sent(lon_copy, 2, send_d, recv_d, j, lons)
    exchange_sent(lat_copy, 0, send_b, recv_b, i, lats)
    exchange_sent(lat_copy, 1, send_e, recv_e, i, lats)
    for d in range(1, zs):
        z_copy(d, z).wait_send()
    for turn in range(zs):
        for d in range(1, lats):
            spread_copy(d, i, lax.rem(z + zs - turn, zs), turn).wait_send()
    for q in range(lats):
        side_copy(side, q).wait_send()
    for q in range(lats):
        side_copy(1 - side, q).wait_recv()
        leaving.append(
            pltpu.make_async_copy(
                gather.at[1 - side, q], gather_out.at[1 - side, q], local_sem.at[12 + q]
            )
        )
        leaving[-1].start()
    for store in leaving:
        store.wait()


def fused_device(fields, spec_cotangent, inner_kernel, inner_offset, outer_kernel, outer_offset):
    lats = lax.axis_size("lat")
    lons = lax.axis_size("lon")
    _, h_local, w_local, channels = fields.shape
    m_local, k_local = spec_cotangent.shape[2:4]
    blocks, width = inner_kernel.shape[1:3]
    height, full_width = h_local * lats, w_local * lons
    wavenumbers = k_local * lats
    lanes = 128
    tokens = height * k_local
    part_rows = m_local * k_local
    deep = width * width // lanes + 8
    normalizer = 1.0 / math.sqrt(height * wavenumbers)
    cols = jnp.asarray(column_tables(full_width, wavenumbers, lats))
    rows, unscale = row_tables(height, k_local)
    rows = jnp.asarray(rows)
    hbm = pl.BlockSpec(memory_space=pltpu.HBM)
    bf16, f32 = jnp.bfloat16, jnp.float32
    wide = (tokens, 2 * lanes)
    dma = pltpu.SemaphoreType.DMA

    def pair(*shape):
        return [pltpu.VMEM(shape, bf16)] * 2

    gathered, arrived = pl.pallas_call(
        lambda *refs: fused_kernel(
            (lats, lons, blocks, width, lanes, normalizer, unscale), *refs
        ),
        name="fused_filter",
        out_shape=[
            jax.ShapeDtypeStruct((2, lats, lons // 2, deep, lanes), bf16),
            jax.ShapeDtypeStruct((blocks, part_rows // 2, 4 * width), bf16),
        ],
        in_specs=[hbm] * 8,
        out_specs=[hbm] * 2,
        scratch_shapes=[
            pltpu.VMEM((2, lats, lons // 2, deep, lanes), bf16),
            pltpu.VMEM((blocks, part_rows // 2, 4 * width), bf16),
            *pair(blocks, w_local, h_local * width),
            *pair(lats, h_local * k_local, 4 * width),
            *pair(blocks, part_rows // 2, 4 * width),
            pltpu.VMEM((blocks, part_rows // 2, 4 * width), bf16),
            *pair(4, deep, lanes),
            *[pltpu.VMEM(wide, bf16)] * 4,
            pltpu.VMEM((4, width, width), bf16),
            *pair(2 * lanes, 2 * lanes),
            pltpu.VMEM(rows.shape, bf16),
            pltpu.VMEM(cols.shape, bf16),
            pltpu.VMEM(fields.shape[1:], bf16),
            pltpu.VMEM((2, m_local, k_local, channels), bf16),
            pltpu.VMEM(inner_offset.shape, f32),
            pltpu.VMEM(outer_offset.shape, f32),
            dma((3, lons)),
            dma((3, lons)),
            dma((2, lats)),
            dma((2, lats)),
            dma((lons // 2,)),
            dma((lons // 2,)),
            dma((lons // 2, lats)),
            dma((lons // 2, lats)),
            dma((lats,)),
            dma((lats,)),
            dma((12 + lats,)),
        ],
        compiler_params=pltpu.CompilerParams(
            collective_id=0, has_side_effects=True, vmem_limit_bytes=63 * 1024 * 1024
        ),
    )(
        fields.reshape(fields.shape[1:]),
        spec_cotangent.reshape(2, m_local, k_local, channels),
        inner_kernel,
        inner_offset,
        outer_kernel,
        outer_offset,
        cols,
        rows,
    )
    filt, inner_grad, inner_bias, outer_grad, outer_bias = pl.pallas_call(
        unpack_kernel,
        name="unpack",
        out_shape=[
            jax.ShapeDtypeStruct((2, m_local, k_local, channels), f32),
            jax.ShapeDtypeStruct(inner_kernel.shape, f32),
            jax.ShapeDtypeStruct(inner_offset.shape, f32),
            jax.ShapeDtypeStruct(outer_kernel.shape, f32),
            jax.ShapeDtypeStruct(outer_offset.shape, f32),
        ],
        in_specs=[hbm] * 2,
        out_specs=[hbm] * 5,
        scratch_shapes=[
            pltpu.VMEM(gathered.shape, bf16),
            pltpu.VMEM(arrived.shape, bf16),
            pltpu.VMEM((2, m_local, k_local, channels), f32),
            pltpu.VMEM((4, blocks, width, width), f32),
            pltpu.VMEM((4, blocks, width), f32),
            dma((20,)),
        ],
        compiler_params=pltpu.CompilerParams(vmem_limit_bytes=63 * 1024 * 1024),
    )(gathered, arrived)
    return (
        filt.reshape(spec_cotangent.shape),
        inner_grad,
        inner_bias,
        outer_grad,
        outer_bias,
    )


def choose_device(fields, spec_cotangent, inner_kernel, *rest):
    lats, lons = lax.axis_size("lat"), lax.axis_size("lon")
    blocks, width = inner_kernel.shape[1:3]
    fits = (
        fields.shape[0] == 1
        and lons == blocks
        and lats == 4
        and width == 96
        and fields.shape[1] == 16
        and fields.shape[2] == 8
        and spec_cotangent.shape[2] == 8
        and spec_cotangent.shape[3] == 8
    )
    chosen = fused_device if fits else per_device
    return chosen(fields, spec_cotangent, inner_kernel, *rest)


def solution(mesh):
    placed = (P(None, "lat", "lon", None), P(None, None, "lon", "lat", None), P(), P(), P(), P())
    return jax.shard_map(
        choose_device,
        mesh=mesh,
        in_specs=placed,
        out_specs=(P(None, None, "lon", "lat", None), P(), P(), P(), P()),
        check_vma=False,
    )
```
